512 devices in a mesh: seq: 16 (over z), exp: 32 (over y, x, core).
Axes of the slice: x: 4, y: 4, z: 16, core: 2. Of those that a mesh axis runs over, the one named last changes fastest.
Arguments:
- byte_embed: bfloat16 [32, 2048, 1024], P('exp', 'seq'), may hold values from -16 to 16
- score_weight: float32 [1024], replicated, may hold values from -1 to 1
- norm_gain: float32 [1024], replicated, may hold values from 0.25 to 1.75
- router: bfloat16 [1024, 32], replicated, may hold values from -0.1875 to 0.1875
- routes: int32 [32, 512, 2], P('exp', 'seq'), may hold values from 0 to 31, all different within a row; in each aligned block of 32 rows (0 to 31, 32 to 63, ..., all dimensions but the last counted through in order) at most 3 rows name the same one
- expert_in: bfloat16 [32, 1024, 4096], P('exp', None, 'seq'), may hold values from -0.1875 to 0.1875
- expert_out: bfloat16 [32, 4096, 1024], P('exp', 'seq'), may hold values from -0.09375 to 0.09375
- cotangent: bfloat16 [32, 512, 1024], P('exp', 'seq'), may hold values from -6 to 6
Outputs:
- grad_embed: bfloat16 [32, 2048, 1024], P('exp', 'seq')
- grad_in: float32 [32, 1024, 4096], P('exp', None, 'seq')
- grad_out: float32 [32, 4096, 1024], P('exp', 'seq')
The draws below stay inside these ranges and needn't reach their ends.
Inputs may be any that keep to these rules, and one draw needn't show every extreme that they name: `routes`: among the 32 tokens of one device, at most 3 pairs name the same expert, and some device reaches 3 for some expert. The two experts of a token differ.
All inputs are finite; a program needn't handle non-finite values.
Results may differ from the reference program's by a relative error of at most 0.014.
Values may be sent and summed in bfloat16 or wider, within the bound.
A program may use at most 64 MiB of HBM per device.

```python
import math
import jax
import jax.numpy as jnp
import numpy as np
from jax import lax

D = 1024
FF = 4096
EXPERTS = 32
TOK_DEV = 32
DOCS = 32
LENGTH = 2048
TOK_DOC = 512
CAP = 3
N_SEQ = 16


def shared_score(key):
    raw = jax.random.truncated_normal(jax.random.fold_in(key, 11), -4.0, 4.0, (D,), jnp.float32)
    return raw * D ** (-0.5)


def draw_score_weight(key, part):
    return shared_score(key)


def draw_byte_embed(key, part):
    shape = (DOCS, LENGTH, D)
    return jax.random.truncated_normal(jax.random.fold_in(key, 1), -4.0, 4.0, shape, jnp.float32).astype(jnp.bfloat16)


def block_scale(rng, dims, cuts, low, high):
    def one(axis_at, blocks):
        steps = jax.random.uniform(jax.random.fold_in(jax.random.fold_in(rng, 6), axis_at), (blocks,), jnp.float32, low / len(cuts), high / len(cuts))
        return jnp.repeat(jnp.exp(steps), dims[axis_at] // blocks).reshape((-1,) + (1,) * (len(dims) - axis_at - 1))

    level = one(*cuts[0])
    for cut in cuts[1:]:
        level = level * one(*cut)
    return level


def assign_block(own_key, own, number, rows, amount, top, reach, skew):
    order = jax.random.permutation(own_key, amount)
    packed, usual = load_shares(amount, rows * top, reach, skew, True), load_shares(amount, rows * top, reach, skew, False)
    places = jnp.arange(amount)

    def named(lengths, turn):
        used = int((lengths > 0).sum())
        fixed = max(1, used // 4)
        moved = fixed + (places - fixed + turn * (used - fixed)) % max(1, amount - fixed)
        return jnp.zeros((amount,), jnp.int32).at[order[jnp.where(places < fixed, places, moved)]].set(jnp.asarray(lengths, jnp.int32))

    lengths = jnp.where(number % 4 == 0, named(packed, number // 4), named(usual, number - number // 4 - 1))
    mixed = jax.random.permutation(jax.random.fold_in(own, 3), amount)
    giver, taker = mixed[0:amount // 2 * 2:2], mixed[1:amount // 2 * 2:2]
    margin = jnp.minimum(lengths[giver] - 1, reach - lengths[taker]) // 2
    margin = jnp.where((giver == order[0]) | (taker == order[0]) | (lengths[taker] == 0), 0, jnp.maximum(margin, 0))
    moved = jax.random.randint(jax.random.fold_in(own, 4), (amount // 2,), 0, 1 << 20) % (margin + 1)
    lengths = lengths.at[giver].add(-moved).at[taker].add(moved)
    members = jnp.searchsorted(jnp.cumsum(lengths), jnp.arange(rows * top), side="right").astype(jnp.int32)
    grid = members.reshape(top, rows).T
    grid = grid[jax.random.permutation(jax.random.fold_in(own, 1), rows)]
    turn = jax.random.randint(jax.random.fold_in(own, 2), (rows, 1), 0, top)
    return jnp.take_along_axis(grid, (jnp.arange(top)[None, :] + turn) % top, axis=1)


def load_shares(amount, total, bound, slope, full):
    portions = [(1 << 20) // math.isqrt(rank ** slope) + 1 for rank in range(1, amount + 1)]
    largest = bound if full else min(bound, max(-(-total // amount), total * portions[0] // sum(portions)))
    least = 1 if total - largest >= amount - 1 else 0
    given, spare = [largest] + [least] * (amount - 1), total - largest - least * (amount - 1)
    while spare > 0:
        candidates = [i for i in range(1, amount) if given[i] < largest] or [i for i in range(1, amount) if given[i] < bound]
        pool, remaining = sum([portions[i] for i in candidates]), spare
        for i in candidates:
            extra = min(bound - given[i], max(1, remaining * portions[i] // pool), spare)
            given[i] = given[i] + extra
            spare = spare - extra
    return np.array(given)


def gaussian(own_key, shape, spread, reach, cuts=(), held_as=jnp.bfloat16):
    result = jax.random.normal(own_key, shape, jnp.float32) * spread
    if len(cuts) > 0:
        result = block_scale(own_key, shape, cuts, -0.22, 0.18) * result
    return jnp.clip(result, min=-reach, max=reach).astype(held_as)


def setup_inputs(seed: int = 0) -> dict:
    seeds = jax.random.split(jax.random.key(seed), 9)
    byte_embed = draw_byte_embed(jax.random.fold_in(seeds[8], 71), 0)
    score_weight = draw_score_weight(jax.random.fold_in(seeds[8], 71), 0)
    norm_gain = jnp.clip(1.0 + 0.15 * jax.random.normal(seeds[2], (D,), jnp.float32), 0.25, 1.75)
    router = gaussian(seeds[3], (D, EXPERTS), D ** -0.5, 0.1875)
    routes_keys = jax.random.split(jax.random.fold_in(seeds[4], 1), DOCS * TOK_DOC // TOK_DEV)
    routes_turns = jax.random.permutation(jax.random.fold_in(seeds[4], 3), DOCS * TOK_DOC // TOK_DEV)
    routes = jax.vmap(lambda own, number: assign_block(jax.random.fold_in(seeds[4], 2), own, number, TOK_DEV, EXPERTS, 2, CAP, 2))(routes_keys, routes_turns).reshape((DOCS, TOK_DOC, 2))
    expert_in = gaussian(seeds[5], (EXPERTS, D, FF), D ** -0.5, 0.1875, ((0, 32), (2, 16)))
    expert_out = gaussian(seeds[6], (EXPERTS, FF, D), FF ** -0.5, 0.09375, ((0, 32), (1, 16)))
    cotangent = gaussian(seeds[7], (DOCS, TOK_DOC, D), 1.0, 6.0, ((0, 32), (1, 16)))
    return dict(byte_embed=byte_embed, score_weight=score_weight, norm_gain=norm_gain, router=router, routes=routes, expert_in=expert_in, expert_out=expert_out, cotangent=cotangent)


SQRT_HALF = 0.7071067811865476
INV_ROOT_TWO_PI = 0.3989422804014327

def front(inputs, norm_gain, score_weight, router, routes):
    batches, length, features = inputs.shape
    highest = lax.Precision.HIGHEST
    quartets = inputs.reshape(batches, length // 4, 4, features)
    pair_means = quartets.reshape(batches, length // 4, 2, 2, features).mean(axis=3)
    quad_mean = quartets.mean(axis=2)
    score_one = jnp.einsum('btqd,d->btq', quartets, score_weight, precision=highest)
    score_two = jnp.repeat(jnp.einsum('btpd,d->btp', pair_means, score_weight, precision=highest), 2, axis=2)
    score_four = jnp.broadcast_to(jnp.einsum('btd,d->bt', quad_mean, score_weight, precision=highest)[:, :, None], score_one.shape)
    largest = jnp.maximum(jnp.maximum(score_one, score_two), score_four)
    weight_one = jnp.exp(score_one - largest)
    weight_two = jnp.exp(score_two - largest)
    weight_four = jnp.exp(score_four - largest)
    denominator = weight_one + weight_two + weight_four
    pair_full = jnp.repeat(pair_means, 2, axis=2)
    blended = (weight_one[..., None] * quartets + weight_two[..., None] * pair_full + weight_four[..., None] * quad_mean[:, :, None, :]) / denominator[..., None]
    tokens = blended.mean(axis=2)
    mean_square = lax.optimization_barrier(jnp.mean(tokens * tokens, axis=-1, keepdims=True))
    normed = tokens * lax.rsqrt(mean_square + 1e-06) * norm_gain
    logits = jnp.einsum('btd,de->bte', normed, router.astype(jnp.float32), precision=highest)
    experts = logits.shape[-1]
    sigmoid_all = 1.0 / (1.0 + jnp.exp(-logits))
    chosen = (routes[..., None] == jnp.arange(experts, dtype=jnp.int32)).astype(jnp.float32)
    picked = lax.optimization_barrier(jnp.sum(chosen * sigmoid_all[:, :, None, :], axis=-1))
    gate_values = picked / lax.optimization_barrier(jnp.sum(picked, axis=-1, keepdims=True))
    return (tokens, normed, gate_values)

def reference(byte_embed, score_weight, norm_gain, router, routes, expert_in, expert_out, cotangent):
    blocks = DOCS * N_SEQ
    slot_total = EXPERTS * blocks * CAP

    def forward_doc(pieces):
        embed_doc, routes_doc = pieces
        tokens, normed, gate_values = front(embed_doc[None].astype(jnp.float32), norm_gain, score_weight, router, routes_doc[None])
        return (normed[0].astype(jnp.bfloat16), gate_values[0])
    normed_all, gate_all = lax.map(forward_doc, (byte_embed, routes))
    token_count = DOCS * TOK_DOC
    normed_flat = normed_all.reshape(token_count, D)
    gate_flat = gate_all.reshape(token_count, 2)
    route_flat = routes.reshape(token_count, 2).astype(jnp.int32)
    cot_flat = cotangent.reshape(token_count, D)
    onehot = (route_flat[:, :, None] == jnp.arange(EXPERTS, dtype=jnp.int32)).astype(jnp.int32)
    running = jnp.cumsum(onehot.reshape(blocks, 2 * TOK_DEV, EXPERTS), axis=1).astype(jnp.int32)
    running = running.reshape(token_count, 2, EXPERTS)
    position = lax.optimization_barrier(jnp.sum(onehot * (running - 1), axis=2)).astype(jnp.int32)
    block_index = (jnp.arange(token_count, dtype=jnp.int32) // TOK_DEV).astype(jnp.int32)
    target = (route_flat * (blocks * CAP) + block_index[:, None] * CAP + position).reshape(-1).astype(jnp.int32)
    source = jnp.repeat(jnp.arange(token_count, dtype=jnp.int32), 2)
    slot_token = jnp.zeros((slot_total,), jnp.int32).at[target].set(source)
    slot_live = jnp.zeros((slot_total,), jnp.float32).at[target].set(1.0)
    slot_gate = jnp.zeros((slot_total,), jnp.float32).at[target].set(gate_flat.reshape(-1)).astype(jnp.bfloat16)
    hidden_share = FF // N_SEQ

    def expert_step(pieces):
        indices, live, gate_rows, weight_in, weight_out = pieces
        row_mask = live.astype(jnp.bfloat16)[:, None]
        token_rows = normed_flat[indices] * row_mask
        cot_rows = cot_flat[indices] * row_mask
        preact = jnp.dot(token_rows, weight_in, preferred_element_type=jnp.float32)
        normal_cdf = 0.5 * (1.0 + jax.scipy.special.erf(preact * SQRT_HALF))
        normal_pdf = INV_ROOT_TWO_PI * jnp.exp(-0.5 * preact * preact)
        hidden = preact * normal_cdf
        upstream = jnp.dot(cot_rows, weight_out.T, preferred_element_type=jnp.float32)
        gate_terms = lax.optimization_barrier(jnp.sum(hidden * upstream, axis=1))
        gate_column = gate_rows.astype(jnp.float32)[:, None]
        hidden_grad = (gate_column * upstream * (normal_cdf + preact * normal_pdf)).astype(jnp.bfloat16)
        gated_hidden = (gate_column * hidden).astype(jnp.bfloat16)
        grad_out = jnp.dot(gated_hidden.T, cot_rows, preferred_element_type=jnp.float32)
        grad_in = jnp.dot(token_rows.T, hidden_grad, preferred_element_type=jnp.float32)
        split_grad = hidden_grad.astype(jnp.float32).reshape(-1, N_SEQ, hidden_share)
        split_weight = weight_in.astype(jnp.float32).reshape(D, N_SEQ, hidden_share)
        partial_rows = jnp.einsum('rsf,dsf->rsd', split_grad, split_weight, precision=lax.Precision.HIGHEST)
        rounded = lax.optimization_barrier(partial_rows.astype(jnp.bfloat16))
        input_rows = lax.optimization_barrier(jnp.sum(rounded.astype(jnp.float32), axis=1)).astype(jnp.bfloat16)
        return (grad_in, grad_out, input_rows, gate_terms.astype(jnp.bfloat16))
    grad_in_all, grad_out_all, input_slots, gate_slots = lax.map(expert_step, (slot_token.reshape(EXPERTS, -1), slot_live.reshape(EXPERTS, -1), slot_gate.reshape(EXPERTS, -1), expert_in, expert_out))
    back_rows = input_slots.reshape(-1, D)[target].reshape(token_count, 2, D)
    normed_grad = lax.optimization_barrier(jnp.sum(back_rows.astype(jnp.float32), axis=1))
    gate_grad = gate_slots.reshape(-1)[target].reshape(token_count, 2).astype(jnp.float32)

    def backward_doc(pieces):
        embed_doc, routes_doc, cot_doc, normed_doc, gate_doc = pieces

        def local_front(values):
            return front(values, norm_gain, score_weight, router, routes_doc[None])
        outputs, pullback = jax.vjp(local_front, embed_doc[None].astype(jnp.float32))
        embed_grad, = pullback((cot_doc[None].astype(jnp.float32), normed_doc[None], gate_doc[None]))
        return embed_grad[0].astype(jnp.bfloat16)
    grad_embed = lax.map(backward_doc, (byte_embed, routes, cotangent, normed_grad.reshape(DOCS, TOK_DOC, D), gate_grad.reshape(DOCS, TOK_DOC, 2)))
    return (grad_embed, grad_in_all, grad_out_all)
```

```python
import functools

import jax
import jax.numpy as jnp
from jax import lax
from jax.experimental import pallas as pl
from jax.experimental.pallas import tpu as pltpu
from jax.sharding import PartitionSpec as P

SQRT_HALF = 0.7071067811865476
INV_ROOT_TWO_PI = 0.3989422804014327
MESH = pl.DeviceIdType.MESH
LANES = 128
SPLIT = 48
ROWS = (((0,), (0,)), ((), ()))
COLS = (((1,), (1,)), ((), ()))
F32 = jnp.float32
BF16 = jnp.bfloat16


def front(inputs, norm_gain, score_weight, router, routes):
    batches, length, features = inputs.shape
    highest = lax.Precision.HIGHEST
    quartets = inputs.reshape(batches, length // 4, 4, features)
    pair_means = quartets.reshape(batches, length // 4, 2, 2, features).mean(axis=3)
    quad_mean = quartets.mean(axis=2)
    score_one = jnp.einsum("btqd,d->btq", quartets, score_weight, precision=highest)
    score_two = jnp.repeat(
        jnp.einsum("btpd,d->btp", pair_means, score_weight, precision=highest), 2, axis=2
    )
    score_four = jnp.broadcast_to(
        jnp.einsum("btd,d->bt", quad_mean, score_weight, precision=highest)[:, :, None],
        score_one.shape,
    )
    largest = jnp.maximum(jnp.maximum(score_one, score_two), score_four)
    weight_one = jnp.exp(score_one - largest)
    weight_two = jnp.exp(score_two - largest)
    weight_four = jnp.exp(score_four - largest)
    denominator = weight_one + weight_two + weight_four
    pair_full = jnp.repeat(pair_means, 2, axis=2)
    blended = (
        weight_one[..., None] * quartets
        + weight_two[..., None] * pair_full
        + weight_four[..., None] * quad_mean[:, :, None, :]
    ) / denominator[..., None]
    tokens = blended.mean(axis=2)
    mean_square = jnp.mean(tokens * tokens, axis=-1, keepdims=True)
    normed = tokens * lax.rsqrt(mean_square + 1e-06) * norm_gain
    logits = jnp.einsum("btd,de->bte", normed, router.astype(F32), precision=highest)
    experts = logits.shape[-1]
    chosen = (routes[..., None] == jnp.arange(experts, dtype=jnp.int32)).astype(F32)
    picked = jnp.sum(chosen * logits[:, :, None, :], axis=-1)
    return (tokens, normed, picked)


def expert_ring(
    steps,
    slots,
    x_ref,
    c_ref,
    win_ref,
    wout_ref,
    gin_ref,
    gout_ref,
    rows_ref,
    gate_ref,
    xs,
    cs,
    hid,
    hgrad,
    part,
    gpart,
    take,
    give,
    gtake,
    ggive,
    ag_send,
    ag_recv,
    rs_send,
    rs_recv,
    rg_send,
    rg_recv,
):
    me = lax.axis_index("seq")
    half = steps // 2
    right = lax.rem(me + 1, steps)
    left = lax.rem(me + steps - 1, steps)
    width = x_ref.shape[1]
    block = width // half

    def rows_of(index, start=0, size=slots):
        return pl.ds(pl.multiple_of(index * slots + start, 16), size)

    def source(way, j):
        return lax.rem(me - j + steps, steps) if way == 0 else lax.rem(me + j, steps)

    def gather(way, j, sub, own=False):
        buf = cs if sub else xs
        place = rows_of(source(way, j))
        src = (c_ref if sub else x_ref) if own else buf.at[place]
        return pltpu.make_async_remote_copy(
            src_ref=src,
            dst_ref=buf.at[place],
            send_sem=ag_send.at[way, j, sub],
            recv_sem=ag_recv.at[way, j, sub],
            device_id={"seq": left if way else right},
            device_id_type=MESH,
        )

    def arrival(way, j, sub):
        buf = cs if sub else xs
        place = rows_of(source(way, j + 1))
        return pltpu.make_async_remote_copy(
            src_ref=buf.at[place],
            dst_ref=buf.at[place],
            send_sem=ag_send.at[way, j, sub],
            recv_sem=ag_recv.at[way, j, sub],
            device_id={"seq": left if way else right},
            device_id_type=MESH,
        )

    def target(way, s):
        return lax.rem(me + half - s, steps) if way == 0 else lax.rem(me + half + s, steps)

    def scatter(way, s, sub, direct=False):
        at = way * half + s
        place = rows_of(at, sub * SPLIT, SPLIT)
        src = part.at[rows_of(target(way, s), sub * SPLIT, SPLIT)] if direct else give.at[place]
        return pltpu.make_async_remote_copy(
            src_ref=src,
            dst_ref=take.at[place],
            send_sem=rs_send.at[way, s, sub],
            recv_sem=rs_recv.at[way, s, sub],
            device_id={"seq": left if way else right},
            device_id_type=MESH,
        )

    def scatter_gate(way, s, direct=False):
        at = way * half + s
        src = gpart.at[target(way, s)] if direct else ggive.at[at]
        return pltpu.make_async_remote_copy(
            src_ref=src,
            dst_ref=gtake.at[at],
            send_sem=rg_send.at[way, s],
            recv_sem=rg_recv.at[way, s],
            device_id={"seq": left if way else right},
            device_id_type=MESH,
        )

    def compute(index):
        place = rows_of(index)
        x = xs[place, :]
        c = cs[place, :]
        pre = jnp.dot(x, win_ref[...], preferred_element_type=F32)
        up = lax.dot_general(c, wout_ref[...], COLS, preferred_element_type=F32)
        cdf = 0.5 * (1.0 + lax.erf(pre * SQRT_HALF))
        pdf = INV_ROOT_TWO_PI * jnp.exp(-0.5 * pre * pre)
        hidden = pre * cdf
        hg = (up * (cdf + pre * pdf)).astype(BF16)
        hid[place, :] = hidden.astype(BF16)
        hgrad[place, :] = hg
        part[place, :] = lax.dot_general(
            hg, win_ref[...], COLS, preferred_element_type=F32
        ).astype(BF16)
        prod = hidden * up
        high = prod.astype(BF16)
        low = (prod - high.astype(F32)).astype(BF16)
        ones = jnp.ones((8, prod.shape[1]), BF16)
        total = lax.dot_general(ones, high, COLS, preferred_element_type=F32)
        total = total + lax.dot_general(ones, low, COLS, preferred_element_type=F32)
        gpart[index, :, 0:slots] = total

    barrier = pltpu.get_barrier_semaphore()
    for peer in (left, right):
        pl.semaphore_signal(barrier, inc=1, device_id={"seq": peer}, device_id_type=MESH)
    pl.semaphore_wait(barrier, 2)

    for sub in range(2):
        for way in range(2):
            gather(way, 0, sub, own=True).start()
    gpart[...] = jnp.zeros_like(gpart)
    xs[rows_of(me), :] = x_ref[...]
    cs[rows_of(me), :] = c_ref[...]
    compute(me)

    def ring_step(j, carry):
        for sub in range(2):
            for way in range(2):
                arrival(way, j - 1, sub).wait_recv()
                gather(way, j, sub).start()
        compute(source(0, j))
        compute(source(1, j))
        return carry

    lax.fori_loop(1, half - 1, ring_step, 0)

    last = half - 1
    for sub in range(2):
        for way in range(2):
            arrival(way, last - 1, sub).wait_recv()
            if sub == way:
                gather(way, last, sub).start()
    compute(source(0, last))
    compute(source(1, last))
    arrival(0, last, 0).wait_recv()
    arrival(1, last, 1).wait_recv()
    compute(source(0, half))

    def weights(s):
        span = pl.ds(pl.multiple_of(s * block, LANES), block)
        gin_ref[span, :] = lax.dot_general(
            xs[:, span], hgrad[...], ROWS, preferred_element_type=F32
        )
        gout_ref[:, span] = lax.dot_general(
            hid[...], cs[:, span], ROWS, preferred_element_type=F32
        )

    def merge(way, s, sub):
        at = way * half + s
        mine = part[rows_of(target(way, s), sub * SPLIT, SPLIT), :].astype(F32)
        came = take[rows_of(at - 1, sub * SPLIT, SPLIT), :].astype(F32)
        give[rows_of(at, sub * SPLIT, SPLIT), :] = (mine + came).astype(BF16)

    scatter(0, 0, 0, direct=True).start()
    scatter(1, 0, 1, direct=True).start()
    scatter_gate(0, 0, direct=True).start()
    scatter(0, 1, 1, direct=True).start()
    scatter(1, 1, 0, direct=True).start()
    scatter_gate(1, 1, direct=True).start()
    weights(0)
    scatter(0, 0, 0, direct=True).wait_recv()
    merge(0, 1, 0)
    scatter(0, 1, 0).start()
    scatter(1, 0, 1, direct=True).wait_recv()
    merge(1, 1, 1)
    scatter(1, 1, 1).start()
    scatter_gate(0, 0, direct=True).wait_recv()
    ggive[1] = gpart[target(0, 1)] + gtake[0]
    scatter_gate(0, 1).start()
    weights(1)

    def scatter_step(s, carry):
        for order in range(2):
            for way in range(2):
                sub = (1 - order) if way == 0 else order
                scatter(way, s - 1, sub).wait_recv()
                merge(way, s, sub)
                scatter(way, s, sub).start()
        for way in range(2):
            scatter_gate(way, s - 1).wait_recv()
            at = way * half + s
            ggive[at] = gpart[target(way, s)] + gtake[at - 1]
            scatter_gate(way, s).start()
        weights(s)
        return carry

    lax.fori_loop(2, half, scatter_step, 0)

    for sub in range(2):
        total = part[rows_of(me, sub * SPLIT, SPLIT), :].astype(F32)
        for way in range(2):
            scatter(way, last, sub).wait_recv()
            total = total + take[rows_of(way * half + last, sub * SPLIT, SPLIT), :].astype(F32)
        rows_ref[pl.ds(sub * SPLIT, SPLIT), :] = total.astype(BF16)
    gate_total = gpart[me]
    for way in range(2):
        scatter_gate(way, last).wait_recv()
        gate_total = gate_total + gtake[way * half + last]
    gate_ref[...] = gate_total

    for way in range(2):
        for sub in range(2):
            gather(way, 0, sub, own=True).wait_send()
    for way in range(2):
        for s in range(half):
            for sub in range(2):
                if s >= 1 and (s < last or sub == way):
                    gather(way, s, sub).wait_send()
                if s >= 1 or sub == way:
                    scatter(way, s, sub).wait_send()
            if s >= 1 or way == 0:
                scatter_gate(way, s).wait_send()


def run_ring(x_rows, c_rows, weight_in, weight_out):
    steps = lax.axis_size("seq")
    slots, width = x_rows.shape
    hidden = weight_in.shape[1]
    half = steps // 2
    vmem = pl.BlockSpec(memory_space=pltpu.VMEM)
    return pl.pallas_call(
        functools.partial(expert_ring, steps, slots),
        out_shape=(
            jax.ShapeDtypeStruct((width, hidden), F32),
            jax.ShapeDtypeStruct((hidden, width), F32),
            jax.ShapeDtypeStruct((slots, width), BF16),
            jax.ShapeDtypeStruct((8, LANES), F32),
        ),
        in_specs=[vmem] * 4,
        out_specs=(vmem,) * 4,
        scratch_shapes=[
            pltpu.VMEM((steps * slots, width), BF16),
            pltpu.VMEM((steps * slots, width), BF16),
            pltpu.VMEM((steps * slots, hidden), BF16),
            pltpu.VMEM((steps * slots, hidden), BF16),
            pltpu.VMEM((steps * slots, width), BF16),
            pltpu.VMEM((steps, 8, LANES), F32),
            pltpu.VMEM((steps * slots, width), BF16),
            pltpu.VMEM((steps * slots, width), BF16),
            pltpu.VMEM((steps, 8, LANES), F32),
            pltpu.VMEM((steps, 8, LANES), F32),
            pltpu.SemaphoreType.DMA((2, half, 2)),
            pltpu.SemaphoreType.DMA((2, half, 2)),
            pltpu.SemaphoreType.DMA((2, half, 2)),
            pltpu.SemaphoreType.DMA((2, half, 2)),
            pltpu.SemaphoreType.DMA((2, half)),
            pltpu.SemaphoreType.DMA((2, half)),
        ],
        compiler_params=pltpu.CompilerParams(
            collective_id=0, has_side_effects=True, vmem_limit_bytes=48 * 1024 * 1024
        ),
    )(x_rows, c_rows, weight_in, weight_out)


def per_device(
    byte_embed, score_weight, norm_gain, router, routes, expert_in, expert_out, cotangent
):
    experts_all = router.shape[1]
    token_count = routes.shape[1]
    width_model = byte_embed.shape[2]
    capacity = max(2, 3 * token_count // experts_all)
    slots = experts_all * capacity
    highest = lax.Precision.HIGHEST

    def local_front(values):
        return front(values, norm_gain, score_weight, router, routes)

    (tokens, normed, picked), pullback = jax.vjp(local_front, byte_embed.astype(F32))
    sigmoids = 1.0 / (1.0 + jnp.exp(-picked[0]))
    gates = sigmoids / jnp.sum(sigmoids, axis=-1, keepdims=True)
    normed_rows = normed[0].astype(BF16)
    route_rows = routes[0]
    onehot = (route_rows[:, :, None] == jnp.arange(experts_all, dtype=jnp.int32)).astype(jnp.int32)
    running = jnp.cumsum(onehot.reshape(2 * token_count, experts_all), axis=0)
    running = running.reshape(token_count, 2, experts_all)
    position = jnp.sum(onehot * (running - 1), axis=2)
    slot_index = route_rows * capacity + position
    matches = (slot_index[:, :, None] == jnp.arange(slots, dtype=jnp.int32)).astype(F32)
    picker = jnp.sum(matches, axis=1).astype(BF16)
    gate_buffer = jnp.sum(jnp.sum(matches * gates[:, :, None], axis=1), axis=0)
    token_buffer = lax.dot_general(picker, normed_rows, ROWS, preferred_element_type=F32)
    cot_buffer = lax.dot_general(picker, cotangent[0], ROWS, preferred_element_type=F32)
    cot_buffer = cot_buffer * gate_buffer[:, None]
    row_buffer = (
        jnp.stack([token_buffer, cot_buffer])
        .astype(BF16)
        .reshape(2, experts_all, capacity, width_model)
    )
    owned = lax.all_to_all(row_buffer, "exp", split_axis=1, concat_axis=1, tiled=True)
    owned = owned.reshape(2, slots, width_model)
    grad_in, grad_out, own_rows, own_terms = run_ring(
        owned[0], owned[1], expert_in[0], expert_out[0]
    )
    extra = jnp.broadcast_to(own_terms[0, :slots].astype(BF16)[:, None], (slots, LANES))
    back = jnp.concatenate([own_rows, extra], axis=1).reshape(experts_all, capacity, -1)
    returned = lax.all_to_all(back, "exp", split_axis=0, concat_axis=0, tiled=True)
    returned = returned.reshape(slots, width_model + LANES)
    normed_grad = jnp.dot(picker, returned[:, :width_model], preferred_element_type=F32)
    scaled = jnp.einsum(
        "tks,s->tk", matches, returned[:, width_model].astype(F32), precision=highest
    )
    picked_grad = (1.0 - sigmoids) * (scaled - gates * jnp.sum(scaled, axis=-1, keepdims=True))
    (embed_grad,) = pullback((cotangent.astype(F32), normed_grad[None], picked_grad[None]))
    return (embed_grad.astype(BF16), grad_in[None], grad_out[None])


def solution(mesh):
    in_specs = (
        P("exp", "seq", None),
        P(),
        P(),
        P(),
        P("exp", "seq", None),
        P("exp", None, "seq"),
        P("exp", "seq", None),
        P("exp", "seq", None),
    )
    out_specs = (P("exp", "seq", None), P("exp", None, "seq"), P("exp", "seq", None))
    return jax.shard_map(
        per_device, mesh=mesh, in_specs=in_specs, out_specs=out_specs, check_vma=False
    )
```

```python
import functools

import jax
import jax.numpy as jnp
from jax import lax
from jax.experimental import pallas as pl
from jax.experimental.pallas import tpu as pltpu
from jax.sharding import PartitionSpec as P

SQRT_HALF = 0.7071067811865476
INV_ROOT_TWO_PI = 0.3989422804014327
MESH = pl.DeviceIdType.MESH
LANES = 128
SPLIT = 48
CAP = 3
GROUP = 16
ROWS = (((0,), (0,)), ((), ()))
COLS = (((1,), (1,)), ((), ()))
F32 = jnp.float32
BF16 = jnp.bfloat16


def pieces(value, count):
    out = []
    for _ in range(count):
        part = value.astype(BF16)
        out.append(part)
        value = value - part.astype(F32)
    return out


def stacked(value):
    parts = [value[:, at : at + LANES] for at in range(0, value.shape[1], LANES)]
    return jnp.concatenate(parts, axis=0)


def unstacked(value, rows):
    parts = [value[at : at + rows, :] for at in range(0, value.shape[0], rows)]
    return jnp.concatenate(parts, axis=1)


def total(value):
    return jnp.sum(value, axis=1, keepdims=True)


def iota(shape, dim):
    return lax.broadcasted_iota(jnp.int32, shape, dim)


def onehot(mask):
    return mask.astype(F32).astype(BF16)


def block_step(
    steps,
    peers,
    emb_hbm,
    score_ref,
    gain_ref,
    router_ref,
    routes_ref,
    win_hbm,
    wout_hbm,
    cot_hbm,
    gemb_ref,
    gin_ref,
    gout_ref,
    emb_ref,
    cot_ref,
    win_ref,
    wout_ref,
    value_ref,
    token_ref,
    send_ref,
    recv_ref,
    bsend_ref,
    brecv_ref,
    sel_ref,
    pick_ref,
    xs,
    cs,
    hid,
    hgrad,
    part,
    gpart,
    take,
    give,
    gtake,
    ggive,
    in_sem,
    fx_send,
    fx_recv,
    bx_send,
    bx_recv,
    ag_send,
    ag_recv,
    rs_send,
    rs_recv,
    rg_send,
    rg_recv,
):
    me = lax.axis_index("seq")
    mine = lax.axis_index("exp")
    half = steps // 2
    right = lax.rem(me + 1, steps)
    left = lax.rem(me + steps - 1, steps)
    tokens_here, width = cot_ref.shape
    slots = peers * CAP
    parts = width // LANES
    block = width // half

    loads = [
        pltpu.make_async_copy(src, dst, in_sem.at[at])
        for at, (src, dst) in enumerate(
            ((emb_hbm, emb_ref), (cot_hbm, cot_ref), (win_hbm, win_ref), (wout_hbm, wout_ref))
        )
    ]
    for load in loads:
        load.start()

    barrier = pltpu.get_barrier_semaphore()
    for peer in (left, right):
        pl.semaphore_signal(barrier, inc=1, device_id={"seq": peer}, device_id_type=MESH)

    def greet(k, carry):
        pl.semaphore_signal(
            barrier, inc=1, device_id={"exp": lax.rem(mine + k, peers)}, device_id_type=MESH
        )
        return carry

    lax.fori_loop(1, peers, greet, 0)

    loads[0].wait()
    loads[1].wait()
    count = 4 * tokens_here
    order = iota((count, count), 0)
    place = iota((count, count), 1)
    shuffle = onehot(place == lax.rem(order, tokens_here) * 4 + order // tokens_here)
    value_ref[...] = jnp.dot(shuffle, emb_ref[...], preferred_element_type=F32)
    values = [value_ref[pl.ds(i * tokens_here, tokens_here), :] for i in range(4)]
    weight = score_ref[...]
    scores = [total(v * weight) for v in values]
    pair = [0.5 * (scores[0] + scores[1]), 0.5 * (scores[2] + scores[3])]
    quad = 0.5 * (pair[0] + pair[1])
    shares = []
    for i in range(4):
        three = (scores[i], pair[i // 2], quad)
        top = jnp.maximum(jnp.maximum(three[0], three[1]), three[2])
        raised = [jnp.exp(s - top) for s in three]
        bottom = raised[0] + raised[1] + raised[2]
        shares.append([r / bottom for r in raised])
    pair_share = [shares[2 * h][1] + shares[2 * h + 1][1] for h in range(2)]
    quad_share = shares[0][2] + shares[1][2] + shares[2][2] + shares[3][2]
    mix = [
        0.25 * (shares[i][0] + 0.5 * pair_share[i // 2] + 0.25 * quad_share) for i in range(4)
    ]
    token = mix[0] * values[0] + mix[1] * values[1] + mix[2] * values[2] + mix[3] * values[3]
    token_ref[...] = token
    scale = lax.rsqrt(total(token * token) * (1.0 / width) + 1e-06)
    normed = token * scale * gain_ref[...]
    sent = normed.astype(BF16)
    router = router_ref[...]
    logits = jnp.zeros((tokens_here, peers), F32)
    for piece in pieces(normed, 3):
        logits = logits + jnp.dot(piece, router, preferred_element_type=F32)
    lane = iota((tokens_here, peers), 1)
    chosen = [lane == routes_ref[:, k : k + 1] for k in range(2)]
    picked = [total(jnp.where(hit, logits, 0.0)) for hit in chosen]
    sigmoids = [1.0 / (1.0 + jnp.exp(-v)) for v in picked]
    gates = [s / (sigmoids[0] + sigmoids[1]) for s in sigmoids]
    named = onehot(chosen[0]) + onehot(chosen[1])
    before = onehot(iota((tokens_here, tokens_here), 1) < iota((tokens_here, tokens_here), 0))
    earlier = jnp.dot(before, named, preferred_element_type=F32)
    spots = [total(jnp.where(hit, earlier, 0.0)).astype(jnp.int32) for hit in chosen]
    codes = [routes_ref[:, k : k + 1] * 4 + spots[k] for k in range(2)]

    tall = parts * tokens_here
    long = peers * GROUP
    column = iota((tall, long), 1)
    expert = column // GROUP
    inner = lax.rem(column, GROUP)
    upper = inner // 8
    piece_at = lax.rem(inner, 8)
    row_piece = iota((tall, 1), 0) // tokens_here
    row_codes = [jnp.concatenate([code] * parts, axis=0) * 8 + row_piece for code in codes]
    row_gates = [jnp.concatenate([gate] * parts, axis=0) for gate in gates]
    base = expert * 32 + piece_at
    wanted = (
        base + upper * 8,
        jnp.where(upper == 0, base + 16, -1),
        jnp.where(upper == 1, base, -1),
        base + 8 + upper * 8,
    )
    for at in range(2):
        hit = jnp.where(row_codes[0] == wanted[at], 1.0, 0.0)
        hit = hit + jnp.where(row_codes[1] == wanted[at], 1.0, 0.0)
        sel_ref[at] = hit.astype(BF16)
    sent_tall = stacked(sent)
    cot_tall = stacked(cot_ref[...])
    own = []
    for at in range(2):
        own.append(lax.dot_general(sel_ref[at], sent_tall, ROWS, preferred_element_type=F32))
    for at in range(2, 4):
        gated = jnp.where(row_codes[0] == wanted[at], row_gates[0], 0.0)
        gated = gated + jnp.where(row_codes[1] == wanted[at], row_gates[1], 0.0)
        high, low = pieces(gated, 2)
        one = lax.dot_general(high, cot_tall, ROWS, preferred_element_type=F32)
        own.append(one + lax.dot_general(low, cot_tall, ROWS, preferred_element_type=F32))
    send_ref[:, 0:LANES] = own[0].astype(BF16)
    send_ref[:, LANES : 2 * LANES] = (own[1] + own[2]).astype(BF16)
    send_ref[:, 2 * LANES : 3 * LANES] = own[3].astype(BF16)

    pl.semaphore_wait(barrier, peers + 1)

    def group_rows(index):
        return pl.ds(pl.multiple_of(index * GROUP, GROUP), GROUP)

    def exchange(k, src_ref, dst_ref, send_sem, recv_sem):
        peer = lax.rem(mine + k, peers)
        return pltpu.make_async_remote_copy(
            src_ref=src_ref.at[group_rows(peer)],
            dst_ref=dst_ref.at[group_rows(mine)],
            send_sem=send_sem.at[k],
            recv_sem=recv_sem.at[k],
            device_id={"exp": peer},
            device_id_type=MESH,
        )

    def arrived(k, src_ref, dst_ref, send_sem, recv_sem):
        peer = lax.rem(mine + peers - k, peers)
        return pltpu.make_async_remote_copy(
            src_ref=src_ref.at[group_rows(peer)],
            dst_ref=dst_ref.at[group_rows(peer)],
            send_sem=send_sem.at[k],
            recv_sem=recv_sem.at[k],
            device_id={"exp": peer},
            device_id_type=MESH,
        )

    def exchange_start(*refs):
        def start(k, carry):
            exchange(k, *refs).start()
            return carry

        lax.fori_loop(1, peers, start, 0)
        refs[1][group_rows(mine), :] = refs[0][group_rows(mine), :]

    def exchange_wait(*refs):
        def wait(k, carry):
            arrived(k, *refs).wait_recv()
            return carry

        lax.fori_loop(1, peers, wait, 0)

    def exchange_end(*refs):
        def wait(k, carry):
            exchange(k, *refs).wait_send()
            return carry

        lax.fori_loop(1, peers, wait, 0)

    forward = (send_ref, recv_ref, fx_send, fx_recv)
    backward = (bsend_ref, brecv_ref, bx_send, bx_recv)
    exchange_start(*forward)

    near = 16
    few = near * CAP
    deep = parts * few
    wide = near * GROUP
    row = iota((deep, wide), 0)
    slot = lax.rem(row, few)
    inner = lax.rem(iota((deep, wide), 1), GROUP)
    same = (slot // CAP == iota((deep, wide), 1) // GROUP) & (lax.rem(inner, 8) == row // few)
    spot = lax.rem(slot, CAP)
    upper = inner // 8
    pick_ref[0] = onehot(same & (spot == upper))
    pick_ref[1] = onehot(same & (spot == 2) & (upper == 0))
    pick_ref[2] = onehot(same & (spot == 0) & (upper == 1))
    pick_ref[3] = onehot(same & (spot == 1 + upper))
    gpart[...] = jnp.zeros_like(gpart)

    def rows_of(index, start=0, size=slots):
        return pl.ds(pl.multiple_of(index * slots + start, 16), size)

    def source(way, j):
        return lax.rem(me - j + steps, steps) if way == 0 else lax.rem(me + j, steps)

    def gather(way, j, sub):
        buf = cs if sub else xs
        at = rows_of(source(way, j))
        return pltpu.make_async_remote_copy(
            src_ref=buf.at[at],
            dst_ref=buf.at[at],
            send_sem=ag_send.at[way, j, sub],
            recv_sem=ag_recv.at[way, j, sub],
            device_id={"seq": left if way else right},
            device_id_type=MESH,
        )

    def arrival(way, j, sub):
        buf = cs if sub else xs
        at = rows_of(source(way, j + 1))
        return pltpu.make_async_remote_copy(
            src_ref=buf.at[at],
            dst_ref=buf.at[at],
            send_sem=ag_send.at[way, j, sub],
            recv_sem=ag_recv.at[way, j, sub],
            device_id={"seq": left if way else right},
            device_id_type=MESH,
        )

    def target(way, s):
        return lax.rem(me + half - s, steps) if way == 0 else lax.rem(me + half + s, steps)

    def scatter(way, s, sub, direct=False):
        at = way * half + s
        here = rows_of(at, sub * SPLIT, SPLIT)
        src = part.at[rows_of(target(way, s), sub * SPLIT, SPLIT)] if direct else give.at[here]
        return pltpu.make_async_remote_copy(
            src_ref=src,
            dst_ref=take.at[here],
            send_sem=rs_send.at[way, s, sub],
            recv_sem=rs_recv.at[way, s, sub],
            device_id={"seq": left if way else right},
            device_id_type=MESH,
        )

    def scatter_gate(way, s, direct=False):
        at = way * half + s
        src = gpart.at[target(way, s)] if direct else ggive.at[at]
        return pltpu.make_async_remote_copy(
            src_ref=src,
            dst_ref=gtake.at[at],
            send_sem=rg_send.at[way, s],
            recv_sem=rg_recv.at[way, s],
            device_id={"seq": left if way else right},
            device_id_type=MESH,
        )

    def compute(index):
        at = rows_of(index)
        pre = jnp.dot(xs[at, :], win_ref[...], preferred_element_type=F32)
        up = lax.dot_general(cs[at, :], wout_ref[...], COLS, preferred_element_type=F32)
        cdf = 0.5 * (1.0 + lax.erf(pre * SQRT_HALF))
        pdf = INV_ROOT_TWO_PI * jnp.exp(-0.5 * pre * pre)
        hidden = pre * cdf
        hg = (up * (cdf + pre * pdf)).astype(BF16)
        hid[at, :] = hidden.astype(BF16)
        hgrad[at, :] = hg
        part[at, :] = lax.dot_general(
            hg, win_ref[...], COLS, preferred_element_type=F32
        ).astype(BF16)
        high, low = pieces(hidden * up, 2)
        ones = jnp.ones((8, high.shape[1]), BF16)
        terms = lax.dot_general(ones, high, COLS, preferred_element_type=F32)
        terms = terms + lax.dot_general(ones, low, COLS, preferred_element_type=F32)
        gpart[index, :, 0:slots] = terms

    exchange_wait(*forward)
    for sub, buf in enumerate((xs, cs)):
        for near_at in range(peers // near):
            here = recv_ref[pl.ds(near_at * wide, wide), :]
            lanes = sub * LANES
            one = jnp.dot(
                pick_ref[2 * sub], here[:, lanes : lanes + LANES], preferred_element_type=F32
            )
            two = jnp.dot(
                pick_ref[2 * sub + 1],
                here[:, lanes + LANES : lanes + 2 * LANES],
                preferred_element_type=F32,
            )
            buf[rows_of(me, near_at * few, few), :] = unstacked((one + two).astype(BF16), few)
        for way in range(2):
            gather(way, 0, sub).start()
    loads[2].wait()
    loads[3].wait()
    compute(me)

    def ring_step(j, carry):
        for sub in range(2):
            for way in range(2):
                arrival(way, j - 1, sub).wait_recv()
                gather(way, j, sub).start()
        compute(source(0, j))
        compute(source(1, j))
        return carry

    lax.fori_loop(1, half - 1, ring_step, 0)

    last = half - 1
    for sub in range(2):
        for way in range(2):
            arrival(way, last - 1, sub).wait_recv()
            if sub == way:
                gather(way, last, sub).start()
    compute(source(0, last))
    compute(source(1, last))
    scatter(0, 1, 1, direct=True).start()
    scatter(1, 1, 0, direct=True).start()
    scatter_gate(1, 1, direct=True).start()
    arrival(0, last, 0).wait_recv()
    arrival(1, last, 1).wait_recv()
    compute(source(0, half))

    def weights(s):
        span = pl.ds(pl.multiple_of(s * block, LANES), block)
        gin_ref[span, :] = lax.dot_general(
            xs[:, span], hgrad[...], ROWS, preferred_element_type=F32
        )
        gout_ref[:, span] = lax.dot_general(
            hid[...], cs[:, span], ROWS, preferred_element_type=F32
        )

    def merge(way, s, sub):
        at = way * half + s
        ours = part[rows_of(target(way, s), sub * SPLIT, SPLIT), :].astype(F32)
        came = take[rows_of(at - 1, sub * SPLIT, SPLIT), :].astype(F32)
        give[rows_of(at, sub * SPLIT, SPLIT), :] = (ours + came).astype(BF16)

    scatter(0, 0, 0, direct=True).start()
    scatter(1, 0, 1, direct=True).start()
    scatter_gate(0, 0, direct=True).start()
    weights(0)
    scatter(0, 0, 0, direct=True).wait_recv()
    merge(0, 1, 0)
    scatter(0, 1, 0).start()
    scatter(1, 0, 1, direct=True).wait_recv()
    merge(1, 1, 1)
    scatter(1, 1, 1).start()
    scatter_gate(0, 0, direct=True).wait_recv()
    ggive[1] = gpart[target(0, 1)] + gtake[0]
    scatter_gate(0, 1).start()
    weights(1)

    def scatter_step(s, carry):
        for order in range(2):
            for way in range(2):
                sub = (1 - order) if way == 0 else order
                scatter(way, s - 1, sub).wait_recv()
                merge(way, s, sub)
                scatter(way, s, sub).start()
        for way in range(2):
            scatter_gate(way, s - 1).wait_recv()
            at = way * half + s
            ggive[at] = gpart[target(way, s)] + gtake[at - 1]
            scatter_gate(way, s).start()
        weights(s)
        return carry

    lax.fori_loop(2, half, scatter_step, 0)

    summed = []
    for sub in range(2):
        whole = part[rows_of(me, sub * SPLIT, SPLIT), :].astype(F32)
        for way in range(2):
            scatter(way, last, sub).wait_recv()
            whole = whole + take[rows_of(way * half + last, sub * SPLIT, SPLIT), :].astype(F32)
        summed.append(whole.astype(BF16))
    terms = gpart[me]
    for way in range(2):
        scatter_gate(way, last).wait_recv()
        terms = terms + gtake[way * half + last]

    for near_at in range(peers // near):
        tall_rows = stacked(summed[near_at])
        here = pl.ds(near_at * wide, wide)
        for at in range(2):
            bsend_ref[here, pl.ds(at * LANES, LANES)] = lax.dot_general(
                pick_ref[at], tall_rows, ROWS, preferred_element_type=F32
            ).astype(BF16)
    row = iota((long, LANES), 0)
    column = iota((long, LANES), 1)
    fits = (column // CAP == row // GROUP) & (
        lax.rem(row, GROUP) == 8 + lax.rem(column, CAP)
    )
    spread = total(jnp.where(fits & (column < slots), terms[0:1, :], 0.0))
    high, low = pieces(spread, 2)
    two = jnp.where(column < LANES // 2, high.astype(F32), low.astype(F32))
    kept = bsend_ref[:, LANES : 2 * LANES].astype(F32)
    bsend_ref[:, LANES : 2 * LANES] = (kept + two).astype(BF16)
    exchange_start(*backward)
    exchange_end(*forward)
    for way in range(2):
        for s in range(half):
            for sub in range(2):
                if s < last or sub == way:
                    gather(way, s, sub).wait_send()
                if s >= 1 or sub == way:
                    scatter(way, s, sub).wait_send()
            if s >= 1 or way == 0:
                scatter_gate(way, s).wait_send()
    exchange_wait(*backward)

    first = brecv_ref[:, 0:LANES]
    second = brecv_ref[:, LANES : 2 * LANES]
    back = jnp.dot(sel_ref[0], first, preferred_element_type=F32)
    back = back + jnp.dot(sel_ref[1], second, preferred_element_type=F32)
    normed_grad = unstacked(back, tokens_here)
    column = iota((tokens_here, long), 1)
    scaled = []
    for k in range(2):
        at = routes_ref[:, k : k + 1] * GROUP + 8 + spots[k]
        found = jnp.dot(onehot(column == at), second, preferred_element_type=F32)
        scaled.append(found[:, 0:1] + found[:, LANES // 2 : LANES // 2 + 1])
    both = scaled[0] + scaled[1]
    logit_grad = jnp.zeros((tokens_here, peers), F32)
    for k in range(2):
        one = (1.0 - sigmoids[k]) * (scaled[k] - gates[k] * both)
        logit_grad = logit_grad + jnp.where(chosen[k], one, 0.0)
    for piece in pieces(logit_grad, 3):
        normed_grad = normed_grad + lax.dot_general(
            piece, router, COLS, preferred_element_type=F32
        )
    token = token_ref[...]
    inner_grad = normed_grad * gain_ref[...]
    slope = total(inner_grad * token) * (scale * scale * scale * (1.0 / width))
    token_grad = cot_ref[...].astype(F32) + inner_grad * scale - token * slope
    values = [value_ref[pl.ds(i * tokens_here, tokens_here), :] for i in range(4)]
    hits = [total(token_grad * v) for v in values]
    pair_hit = [hits[0] + hits[1], hits[2] + hits[3]]
    quad_hit = pair_hit[0] + pair_hit[1]
    score_grads = []
    for i in range(4):
        grads = (0.25 * hits[i], 0.125 * pair_hit[i // 2], 0.0625 * quad_hit)
        mean = sum(a * g for a, g in zip(shares[i], grads))
        score_grads.append([a * (g - mean) for a, g in zip(shares[i], grads)])
    pair_grad = [score_grads[2 * h][1] + score_grads[2 * h + 1][1] for h in range(2)]
    quad_grad = sum(g[2] for g in score_grads)
    result = []
    for i in range(4):
        own_grad = score_grads[i][0] + 0.5 * pair_grad[i // 2] + 0.25 * quad_grad
        result.append((mix[i] * token_grad + own_grad * weight).astype(BF16))
    shuffle = onehot(order == lax.rem(place, tokens_here) * 4 + place // tokens_here)
    gemb_ref[...] = jnp.dot(
        shuffle, jnp.concatenate(result, axis=0), preferred_element_type=F32
    ).astype(BF16)
    exchange_end(*backward)


def per_device(
    byte_embed, score_weight, norm_gain, router, routes, expert_in, expert_out, cotangent
):
    steps, peers = lax.axis_size("seq"), lax.axis_size("exp")
    count, width = byte_embed.shape[1:]
    hidden = expert_in.shape[2]
    tokens_here = routes.shape[1]
    half = steps // 2
    slots = peers * CAP
    long = peers * GROUP
    parts = width // LANES
    vmem = pl.BlockSpec(memory_space=pltpu.VMEM)
    hbm = pl.BlockSpec(memory_space=pl.ANY)
    dma = pltpu.SemaphoreType.DMA
    gemb, gin, gout = pl.pallas_call(
        functools.partial(block_step, steps, peers),
        out_shape=(
            jax.ShapeDtypeStruct((count, width), BF16),
            jax.ShapeDtypeStruct((width, hidden), F32),
            jax.ShapeDtypeStruct((hidden, width), F32),
        ),
        in_specs=[hbm, vmem, vmem, vmem, vmem, hbm, hbm, hbm],
        out_specs=(vmem,) * 3,
        scratch_shapes=[
            pltpu.VMEM((count, width), BF16),
            pltpu.VMEM((tokens_here, width), BF16),
            pltpu.VMEM((width, hidden), BF16),
            pltpu.VMEM((hidden, width), BF16),
            pltpu.VMEM((count, width), F32),
            pltpu.VMEM((tokens_here, width), F32),
            pltpu.VMEM((long, 3 * LANES), BF16),
            pltpu.VMEM((long, 3 * LANES), BF16),
            pltpu.VMEM((long, 2 * LANES), BF16),
            pltpu.VMEM((long, 2 * LANES), BF16),
            pltpu.VMEM((2, parts * tokens_here, long), BF16),
            pltpu.VMEM((4, parts * 16 * CAP, 16 * GROUP), BF16),
            pltpu.VMEM((steps * slots, width), BF16),
            pltpu.VMEM((steps * slots, width), BF16),
            pltpu.VMEM((steps * slots, hidden), BF16),
            pltpu.VMEM((steps * slots, hidden), BF16),
            pltpu.VMEM((steps * slots, width), BF16),
            pltpu.VMEM((steps, 8, LANES), F32),
            pltpu.VMEM((steps * slots, width), BF16),
            pltpu.VMEM((steps * slots, width), BF16),
            pltpu.VMEM((steps, 8, LANES), F32),
            pltpu.VMEM((steps, 8, LANES), F32),
            dma((4,)),
            dma((peers,)),
            dma((peers,)),
            dma((peers,)),
            dma((peers,)),
            dma((2, half, 2)),
            dma((2, half, 2)),
            dma((2, half, 2)),
            dma((2, half, 2)),
            dma((2, half)),
            dma((2, half)),
        ],
        compiler_params=pltpu.CompilerParams(
            collective_id=0, has_side_effects=True, vmem_limit_bytes=52 * 1024 * 1024
        ),
    )(
        byte_embed[0],
        score_weight[None],
        norm_gain[None],
        router,
        routes[0],
        expert_in[0],
        expert_out[0],
        cotangent[0],
    )
    return (gemb[None], gin[None], gout[None])


def solution(mesh):
    in_specs = (
        P("exp", "seq", None),
        P(),
        P(),
        P(),
        P("exp", "seq", None),
        P("exp", None, "seq"),
        P("exp", "seq", None),
        P("exp", "seq", None),
    )
    out_specs = (P("exp", "seq", None), P("exp", None, "seq"), P("exp", "seq", None))
    return jax.shard_map(
        per_device, mesh=mesh, in_specs=in_specs, out_specs=out_specs, check_vma=False
    )
```

```python
import functools

import jax
import jax.numpy as jnp
from jax import lax
from jax.experimental import pallas as pl
from jax.experimental.pallas import tpu as pltpu
from jax.sharding import PartitionSpec as P

SQRT_HALF = 0.7071067811865476
INV_ROOT_TWO_PI = 0.3989422804014327
MESH = pl.DeviceIdType.MESH
LANES = 128
SPLIT = 48
SPREAD = 3
CAP = 3
GROUP = 16
ROWS = (((0,), (0,)), ((), ()))
COLS = (((1,), (1,)), ((), ()))
F32 = jnp.float32
BF16 = jnp.bfloat16


def pieces(value, count):
    out = []
    for _ in range(count):
        part = value.astype(BF16)
        out.append(part)
        value = value - part.astype(F32)
    return out


def stacked(value):
    parts = [value[:, at : at + LANES] for at in range(0, value.shape[1], LANES)]
    return jnp.concatenate(parts, axis=0)


def unstacked(value, rows):
    parts = [value[at : at + rows, :] for at in range(0, value.shape[0], rows)]
    return jnp.concatenate(parts, axis=1)


def total(value):
    return jnp.sum(value, axis=1, keepdims=True)


def iota(shape, dim):
    return lax.broadcasted_iota(jnp.int32, shape, dim)


def onehot(mask):
    return mask.astype(F32).astype(BF16)


def block_step(
    steps,
    peers,
    emb_hbm,
    score_hbm,
    gain_hbm,
    router_hbm,
    routes_hbm,
    win_hbm,
    wout_hbm,
    cot_hbm,
    gemb_ref,
    gin_ref,
    gout_ref,
    emb_ref,
    cot_ref,
    win_ref,
    wout_ref,
    score_ref,
    gain_ref,
    router_ref,
    routes_ref,
    value_ref,
    token_ref,
    send_ref,
    recv_ref,
    bsend_ref,
    brecv_ref,
    sel_ref,
    pick_ref,
    spread_ref,
    tb,
    tsend,
    trecv,
    xs,
    cs,
    hid,
    hgrad,
    part,
    gpart,
    take,
    give,
    gtake,
    ggive,
    in_sem,
    fx_send,
    fx_recv,
    bx_send,
    bx_recv,
    tb_send,
    tb_recv,
    tx_send,
    tx_recv,
    ag_send,
    ag_recv,
    rs_send,
    rs_recv,
    rg_send,
    rg_recv,
):
    me = lax.axis_index("seq")
    mine = lax.axis_index("exp")
    half = steps // 2
    right = lax.rem(me + 1, steps)
    left = lax.rem(me + steps - 1, steps)
    tokens_here, width = cot_ref.shape
    slots = peers * CAP
    parts = width // LANES
    block = width // half
    count_sub = slots // SPLIT
    early = (tuple(range(count_sub // 2)), tuple(range(count_sub // 2, count_sub)))
    fresh = early[::-1]
    wide_cols = SPREAD * LANES
    ring_cols = width - wide_cols

    loads = [
        pltpu.make_async_copy(src, dst, in_sem.at[at])
        for at, (src, dst) in enumerate(
            (
                (emb_hbm, emb_ref),
                (score_hbm, score_ref),
                (gain_hbm, gain_ref),
                (routes_hbm, routes_ref),
                (router_hbm, router_ref),
                (cot_hbm, cot_ref),
                (win_hbm, win_ref),
                (wout_hbm, wout_ref),
            )
        )
    ]
    for load in loads:
        load.start()

    barrier = pltpu.get_barrier_semaphore()
    for peer in (left, right):
        pl.semaphore_signal(barrier, inc=1, device_id={"seq": peer}, device_id_type=MESH)

    def greet(k, carry):
        pl.semaphore_signal(
            barrier, inc=1, device_id={"exp": lax.rem(mine + k, peers)}, device_id_type=MESH
        )
        return carry

    lax.fori_loop(1, peers, greet, 0)

    loads[0].wait()
    loads[1].wait()
    count = 4 * tokens_here
    order = iota((count, count), 0)
    place = iota((count, count), 1)
    shuffle = onehot(place == lax.rem(order, tokens_here) * 4 + order // tokens_here)
    value_ref[...] = jnp.dot(shuffle, emb_ref[...], preferred_element_type=F32)
    values = [value_ref[pl.ds(i * tokens_here, tokens_here), :] for i in range(4)]
    weight = score_ref[...]
    scores = [total(v * weight) for v in values]
    pair = [0.5 * (scores[0] + scores[1]), 0.5 * (scores[2] + scores[3])]
    quad = 0.5 * (pair[0] + pair[1])
    shares = []
    for i in range(4):
        three = (scores[i], pair[i // 2], quad)
        top = jnp.maximum(jnp.maximum(three[0], three[1]), three[2])
        raised = [jnp.exp(s - top) for s in three]
        bottom = raised[0] + raised[1] + raised[2]
        shares.append([r / bottom for r in raised])
    pair_share = [shares[2 * h][1] + shares[2 * h + 1][1] for h in range(2)]
    quad_share = shares[0][2] + shares[1][2] + shares[2][2] + shares[3][2]
    mix = [
        0.25 * (shares[i][0] + 0.5 * pair_share[i // 2] + 0.25 * quad_share) for i in range(4)
    ]
    token = mix[0] * values[0] + mix[1] * values[1] + mix[2] * values[2] + mix[3] * values[3]
    token_ref[...] = token
    scale = lax.rsqrt(total(token * token) * (1.0 / width) + 1e-06)
    for load in loads[2:6]:
        load.wait()
    normed = token * scale * gain_ref[...]
    sent = normed.astype(BF16)
    router = router_ref[...]
    logits = jnp.zeros((tokens_here, peers), F32)
    for piece in pieces(normed, 3):
        logits = logits + lax.dot_general(piece, router, COLS, preferred_element_type=F32)
    lane = iota((tokens_here, peers), 1)
    level = lane == iota((tokens_here, peers), 0)
    named = routes_ref[...].astype(F32)
    routes = [
        total(jnp.where(level, named[k : k + 1, :], 0.0)).astype(jnp.int32) for k in range(2)
    ]
    chosen = [lane == routes[k] for k in range(2)]
    picked = [total(jnp.where(hit, logits, 0.0)) for hit in chosen]
    sigmoids = [1.0 / (1.0 + jnp.exp(-v)) for v in picked]
    gates = [s / (sigmoids[0] + sigmoids[1]) for s in sigmoids]
    named = onehot(chosen[0]) + onehot(chosen[1])
    before = onehot(iota((tokens_here, tokens_here), 1) < iota((tokens_here, tokens_here), 0))
    earlier = jnp.dot(before, named, preferred_element_type=F32)
    spots = [total(jnp.where(hit, earlier, 0.0)).astype(jnp.int32) for hit in chosen]
    codes = [routes[k] * 4 + spots[k] for k in range(2)]

    tall = parts * tokens_here
    long = peers * GROUP
    column = iota((tall, long), 1)
    expert = column // GROUP
    inner = lax.rem(column, GROUP)
    upper = inner // 8
    piece_at = lax.rem(inner, 8)
    row_piece = iota((tall, 1), 0) // tokens_here
    row_codes = [jnp.concatenate([code] * parts, axis=0) * 8 + row_piece for code in codes]
    row_gates = [jnp.concatenate([gate] * parts, axis=0) for gate in gates]
    base = expert * 32 + piece_at
    wanted = (
        base + upper * 8,
        jnp.where(upper == 0, base + 16, -1),
        jnp.where(upper == 1, base, -1),
        base + 8 + upper * 8,
    )
    for at in range(2):
        hit = jnp.where(row_codes[0] == wanted[at], 1.0, 0.0)
        hit = hit + jnp.where(row_codes[1] == wanted[at], 1.0, 0.0)
        sel_ref[at] = hit.astype(BF16)
    sent_tall = stacked(sent)
    cot_tall = stacked(cot_ref[...])
    own = []
    for at in range(2):
        own.append(lax.dot_general(sel_ref[at], sent_tall, ROWS, preferred_element_type=F32))
    for at in range(2, 4):
        gated = jnp.where(row_codes[0] == wanted[at], row_gates[0], 0.0)
        gated = gated + jnp.where(row_codes[1] == wanted[at], row_gates[1], 0.0)
        high, low = pieces(gated, 2)
        one = lax.dot_general(high, cot_tall, ROWS, preferred_element_type=F32)
        own.append(one + lax.dot_general(low, cot_tall, ROWS, preferred_element_type=F32))
    send_ref[:, 0:LANES] = own[0].astype(BF16)
    send_ref[:, LANES : 2 * LANES] = (own[1] + own[2]).astype(BF16)
    send_ref[:, 2 * LANES : 3 * LANES] = own[3].astype(BF16)

    meta = jnp.zeros((tokens_here, LANES), F32)
    lane = iota((tokens_here, LANES), 1)
    for k in range(2):
        high, low = pieces(gates[k], 2)
        for at, column in enumerate((codes[k].astype(F32), high.astype(F32), low.astype(F32))):
            meta = jnp.where(lane == 2 * at + k, column, meta)

    def token_rows(index):
        return pl.ds(pl.multiple_of(index * tokens_here, tokens_here), tokens_here)

    tb[token_rows(me), 0:LANES] = meta.astype(BF16)
    tb[token_rows(me), LANES : LANES + wide_cols] = sent[:, ring_cols:]
    tb[token_rows(me), LANES + wide_cols :] = cot_ref[:, ring_cols:]

    def source(way, j):
        return lax.rem(me - j + steps, steps) if way == 0 else lax.rem(me + j, steps)

    def token_copy(way, j, index):
        cols = pl.ds(0, LANES + 2 * wide_cols)
        if isinstance(j, int) and j == half - 1:
            cols = pl.ds(LANES + wide_cols, wide_cols) if way else pl.ds(0, LANES + wide_cols)
        here = tb.at[token_rows(index), cols]
        return pltpu.make_async_remote_copy(
            src_ref=here,
            dst_ref=here,
            send_sem=tb_send.at[way, j],
            recv_sem=tb_recv.at[way, j],
            device_id={"seq": left if way else right},
            device_id_type=MESH,
        )

    def token_send(way, j):
        return token_copy(way, j, source(way, j))

    def token_arrival(way, j):
        return token_copy(way, j, source(way, j + 1))

    def spread_rows(j, start=0, size=long):
        return pl.ds(pl.multiple_of((j - 1) * long + start, 16), size)

    def spread_copy(j, k):
        peer = lax.rem(mine + k, peers)
        return pltpu.make_async_remote_copy(
            src_ref=tsend.at[spread_rows(j, peer * GROUP, GROUP)],
            dst_ref=trecv.at[spread_rows(j, mine * GROUP, GROUP)],
            send_sem=tx_send.at[j - 1],
            recv_sem=tx_recv.at[j - 1],
            device_id={"exp": peer},
            device_id_type=MESH,
        )

    def spread_all(j):
        size = (peers - 1) * GROUP
        return pltpu.make_async_remote_copy(
            src_ref=tsend.at[spread_rows(j, 0, size)],
            dst_ref=trecv.at[spread_rows(j, 0, size)],
            send_sem=tx_send.at[j - 1],
            recv_sem=tx_recv.at[j - 1],
            device_id={"exp": lax.rem(mine + 1, peers)},
            device_id_type=MESH,
        )

    def choose(index, offset):
        block = tb[token_rows(index), :]
        meta = block[:, 0:LANES].astype(F32)
        column = iota((tokens_here, long), 1)
        row = lax.rem(column, GROUP) - offset
        base = (column // GROUP) * 4
        for_x = jnp.where((row >= 0) & (row < CAP), base + row, -1).astype(F32)
        for_c = jnp.where((row >= CAP) & (row < 2 * CAP), base + row - CAP, -1).astype(F32)
        found = high = low = jnp.zeros((tokens_here, long), F32)
        for k in range(2):
            code = meta[:, k : k + 1]
            found = found + jnp.where(code == for_x, 1.0, 0.0)
            high = high + jnp.where(code == for_c, meta[:, 2 + k : 3 + k], 0.0)
            low = low + jnp.where(code == for_c, meta[:, 4 + k : 5 + k], 0.0)
        cot = block[:, LANES + wide_cols :]
        picks = [found.astype(BF16), high.astype(BF16), low.astype(BF16)]
        return picks, [block[:, LANES : LANES + wide_cols], cot, cot]

    def spread(j):
        picks, rows = choose(source(0, j), 0)
        if not (isinstance(j, int) and j == half):
            more_picks, more_rows = choose(source(1, j), 2 * CAP)
            picks, rows = picks + more_picks, rows + more_rows
        tsend[spread_rows(j), :] = lax.dot_general(
            jnp.concatenate(picks, axis=0),
            jnp.concatenate(rows, axis=0),
            ROWS,
            preferred_element_type=F32,
        ).astype(BF16)

        def start(k, carry):
            spread_copy(j, k).start()
            return carry

        lax.fori_loop(1, peers, start, 0)
        trecv[spread_rows(j, mine * GROUP, GROUP), :] = tsend[
            spread_rows(j, mine * GROUP, GROUP), :
        ]

    def token_step(j):
        for way in range(2):
            token_arrival(way, j - 1).wait_recv()
            if not (isinstance(j, int) and j == half):
                token_send(way, j).start()
        spread(j)

    pl.semaphore_wait(barrier, peers + 1)
    for way in range(2):
        token_send(way, 0).start()

    def group_rows(index):
        return pl.ds(pl.multiple_of(index * GROUP, GROUP), GROUP)

    def exchange(k, src_ref, dst_ref, send_sem, recv_sem):
        peer = lax.rem(mine + k, peers)
        return pltpu.make_async_remote_copy(
            src_ref=src_ref.at[group_rows(peer)],
            dst_ref=dst_ref.at[group_rows(mine)],
            send_sem=send_sem.at[k],
            recv_sem=recv_sem.at[k],
            device_id={"exp": peer},
            device_id_type=MESH,
        )

    def arrived(k, src_ref, dst_ref, send_sem, recv_sem):
        peer = lax.rem(mine + peers - k, peers)
        return pltpu.make_async_remote_copy(
            src_ref=src_ref.at[group_rows(peer)],
            dst_ref=dst_ref.at[group_rows(peer)],
            send_sem=send_sem.at[k],
            recv_sem=recv_sem.at[k],
            device_id={"exp": peer},
            device_id_type=MESH,
        )

    def exchange_start(*refs):
        def start(k, carry):
            exchange(k, *refs).start()
            return carry

        lax.fori_loop(1, peers, start, 0)
        refs[1][group_rows(mine), :] = refs[0][group_rows(mine), :]

    def exchange_wait(*refs):
        def wait(k, carry):
            arrived(k, *refs).wait_recv()
            return carry

        lax.fori_loop(1, peers, wait, 0)

    def exchange_end(*refs):
        def wait(k, carry):
            exchange(k, *refs).wait_send()
            return carry

        lax.fori_loop(1, peers, wait, 0)

    forward = (send_ref, recv_ref, fx_send, fx_recv)
    backward = (bsend_ref, brecv_ref, bx_send, bx_recv)
    exchange_start(*forward)

    near = 16
    few = near * CAP
    deep = parts * few
    wide = near * GROUP
    row = iota((deep, wide), 0)
    slot = lax.rem(row, few)
    inner = lax.rem(iota((deep, wide), 1), GROUP)
    same = (slot // CAP == iota((deep, wide), 1) // GROUP) & (lax.rem(inner, 8) == row // few)
    spot = lax.rem(slot, CAP)
    upper = inner // 8
    pick_ref[0] = onehot(same & (spot == upper))
    pick_ref[1] = onehot(same & (spot == 2) & (upper == 0))
    pick_ref[2] = onehot(same & (spot == 0) & (upper == 1))
    pick_ref[3] = onehot(same & (spot == 1 + upper))
    gpart[...] = jnp.zeros_like(gpart)
    row = iota((4 * few, wide), 0)
    column = iota((4 * few, wide), 1)
    slot = lax.rem(row, few)
    spread_ref[...] = onehot(
        (slot // CAP == column // GROUP)
        & (lax.rem(column, GROUP) == (row // few) * CAP + lax.rem(slot, CAP))
    )

    def rows_of(index, start=0, size=slots):
        return pl.ds(pl.multiple_of(index * slots + start, 16), size)

    def spread_in(j):
        spread_all(j).wait_recv()
        both = not (isinstance(j, int) and j == half)
        for at in range(peers // near):
            found = jnp.dot(
                spread_ref[...],
                trecv[spread_rows(j, at * wide, wide), :],
                preferred_element_type=F32,
            ).astype(BF16)
            for way in range(2 if both else 1):
                here = rows_of(source(way, j), at * few, few)
                base = 2 * way * few
                xs[here, ring_cols:] = found[base : base + few, :]
                cs[here, ring_cols:] = found[base + few : base + 2 * few, :]

    def gather(way, j, sub):
        buf = cs if sub else xs
        at = rows_of(source(way, j))
        return pltpu.make_async_remote_copy(
            src_ref=buf.at[at, pl.ds(0, ring_cols)],
            dst_ref=buf.at[at, pl.ds(0, ring_cols)],
            send_sem=ag_send.at[way, j, sub],
            recv_sem=ag_recv.at[way, j, sub],
            device_id={"seq": left if way else right},
            device_id_type=MESH,
        )

    def arrival(way, j, sub):
        buf = cs if sub else xs
        at = rows_of(source(way, j + 1))
        return pltpu.make_async_remote_copy(
            src_ref=buf.at[at, pl.ds(0, ring_cols)],
            dst_ref=buf.at[at, pl.ds(0, ring_cols)],
            send_sem=ag_send.at[way, j, sub],
            recv_sem=ag_recv.at[way, j, sub],
            device_id={"seq": left if way else right},
            device_id_type=MESH,
        )

    def target(way, s):
        return lax.rem(me + half - s, steps) if way == 0 else lax.rem(me + half + s, steps)

    def scatter(way, s, sub, direct=False):
        at = way * half + s
        here = rows_of(at, sub * SPLIT, SPLIT)
        src = part.at[rows_of(target(way, s), sub * SPLIT, SPLIT)] if direct else give.at[here]
        return pltpu.make_async_remote_copy(
            src_ref=src,
            dst_ref=take.at[here],
            send_sem=rs_send.at[way, s, sub],
            recv_sem=rs_recv.at[way, s, sub],
            device_id={"seq": left if way else right},
            device_id_type=MESH,
        )

    def scatter_gate(way, s, direct=False):
        at = way * half + s
        src = gpart.at[target(way, s)] if direct else ggive.at[at]
        return pltpu.make_async_remote_copy(
            src_ref=src,
            dst_ref=gtake.at[at],
            send_sem=rg_send.at[way, s],
            recv_sem=rg_recv.at[way, s],
            device_id={"seq": left if way else right},
            device_id_type=MESH,
        )

    def compute(index):
        at = rows_of(index)
        pre = jnp.dot(xs[at, :], win_ref[...], preferred_element_type=F32)
        up = lax.dot_general(cs[at, :], wout_ref[...], COLS, preferred_element_type=F32)
        cdf = 0.5 * (1.0 + lax.erf(pre * SQRT_HALF))
        pdf = INV_ROOT_TWO_PI * jnp.exp(-0.5 * pre * pre)
        hidden = pre * cdf
        hg = (up * (cdf + pre * pdf)).astype(BF16)
        hid[at, :] = hidden.astype(BF16)
        hgrad[at, :] = hg
        part[at, :] = lax.dot_general(
            hg, win_ref[...], COLS, preferred_element_type=F32
        ).astype(BF16)
        high, low = pieces(hidden * up, 2)
        ones = jnp.ones((8, high.shape[1]), BF16)
        terms = lax.dot_general(ones, high, COLS, preferred_element_type=F32)
        terms = terms + lax.dot_general(ones, low, COLS, preferred_element_type=F32)
        gpart[index, :, 0:slots] = terms

    token_step(1)
    token_step(2)
    exchange_wait(*forward)
    for sub, buf in enumerate((xs, cs)):
        for near_at in range(peers // near):
            here = recv_ref[pl.ds(near_at * wide, wide), :]
            lanes = sub * LANES
            one = jnp.dot(
                pick_ref[2 * sub], here[:, lanes : lanes + LANES], preferred_element_type=F32
            )
            two = jnp.dot(
                pick_ref[2 * sub + 1],
                here[:, lanes + LANES : lanes + 2 * LANES],
                preferred_element_type=F32,
            )
            buf[rows_of(me, near_at * few, few), :] = unstacked((one + two).astype(BF16), few)
        for way in range(2):
            gather(way, 0, sub).start()
    loads[6].wait()
    loads[7].wait()
    compute(me)

    def pass_on(j):
        for sub in range(2):
            for way in range(2):
                arrival(way, j - 1, sub).wait_recv()
                gather(way, j, sub).start()

    def ring_step(j, carry):
        token_step(j + 2)
        pass_on(j)
        spread_in(j)
        compute(source(0, j))
        compute(source(1, j))
        return carry

    lax.fori_loop(1, half - 3, ring_step, 0)
    last = half - 1
    ring_step(last - 2, 0)
    ring_step(last - 1, 0)
    for sub in range(2):
        for way in range(2):
            arrival(way, last - 1, sub).wait_recv()
            if sub == way:
                gather(way, last, sub).start()
    spread_in(last)
    for way in range(2):
        compute(source(way, last))
        for sub in fresh[1 - way]:
            scatter(1 - way, 1, sub, direct=True).start()
    scatter_gate(1, 1, direct=True).start()
    spread_in(half)
    arrival(0, last, 0).wait_recv()
    arrival(1, last, 1).wait_recv()
    compute(source(0, half))

    def weights(s):
        span = pl.ds(pl.multiple_of(s * block, LANES), block)
        gin_ref[span, :] = lax.dot_general(
            xs[:, span], hgrad[...], ROWS, preferred_element_type=F32
        )
        gout_ref[:, span] = lax.dot_general(
            hid[...], cs[:, span], ROWS, preferred_element_type=F32
        )

    def merge(way, s, sub):
        at = way * half + s
        ours = part[rows_of(target(way, s), sub * SPLIT, SPLIT), :].astype(F32)
        came = take[rows_of(at - 1, sub * SPLIT, SPLIT), :].astype(F32)
        give[rows_of(at, sub * SPLIT, SPLIT), :] = (ours + came).astype(BF16)

    for way in range(2):
        for sub in early[way]:
            scatter(way, 0, sub, direct=True).start()
    scatter_gate(0, 0, direct=True).start()
    weights(0)
    for at in range(len(early[0])):
        for way in range(2):
            sub = early[way][at]
            scatter(way, 0, sub, direct=True).wait_recv()
            merge(way, 1, sub)
            scatter(way, 1, sub).start()
    scatter_gate(0, 0, direct=True).wait_recv()
    ggive[1] = gpart[target(0, 1)] + gtake[0]
    scatter_gate(0, 1).start()
    weights(1)

    def scatter_step(s, carry):
        for at in range(count_sub):
            for way in range(2):
                sub = (fresh[way] + early[way])[at]
                scatter(way, s - 1, sub).wait_recv()
                merge(way, s, sub)
                scatter(way, s, sub).start()
        for way in range(2):
            scatter_gate(way, s - 1).wait_recv()
            at = way * half + s
            ggive[at] = gpart[target(way, s)] + gtake[at - 1]
            scatter_gate(way, s).start()
        weights(s)
        return carry

    lax.fori_loop(2, half, scatter_step, 0)

    summed = []
    for sub in range(count_sub):
        whole = part[rows_of(me, sub * SPLIT, SPLIT), :].astype(F32)
        for way in range(2):
            scatter(way, last, sub).wait_recv()
            whole = whole + take[rows_of(way * half + last, sub * SPLIT, SPLIT), :].astype(F32)
        summed.append(whole.astype(BF16))
    each = count_sub * near // peers
    summed = [jnp.concatenate(summed[at : at + each], axis=0) for at in range(0, count_sub, each)]
    terms = gpart[me]
    for way in range(2):
        scatter_gate(way, last).wait_recv()
        terms = terms + gtake[way * half + last]

    for near_at in range(peers // near):
        tall_rows = stacked(summed[near_at])
        here = pl.ds(near_at * wide, wide)
        for at in range(2):
            bsend_ref[here, pl.ds(at * LANES, LANES)] = lax.dot_general(
                pick_ref[at], tall_rows, ROWS, preferred_element_type=F32
            ).astype(BF16)
    row = iota((long, LANES), 0)
    column = iota((long, LANES), 1)
    fits = (column // CAP == row // GROUP) & (
        lax.rem(row, GROUP) == 8 + lax.rem(column, CAP)
    )
    spread = total(jnp.where(fits & (column < slots), terms[0:1, :], 0.0))
    high, low = pieces(spread, 2)
    two = jnp.where(column < LANES // 2, high.astype(F32), low.astype(F32))
    kept = bsend_ref[:, LANES : 2 * LANES].astype(F32)
    bsend_ref[:, LANES : 2 * LANES] = (kept + two).astype(BF16)
    exchange_start(*backward)
    exchange_end(*forward)
    for way in range(2):
        for s in range(half):
            token_send(way, s).wait_send()
            if way == 0:
                spread_all(s + 1).wait_send()
            for sub in range(2):
                if s < last or sub == way:
                    gather(way, s, sub).wait_send()
            for sub in range(count_sub):
                if s >= 1 or sub in early[way]:
                    scatter(way, s, sub).wait_send()
            if s >= 1 or way == 0:
                scatter_gate(way, s).wait_send()
    exchange_wait(*backward)

    first = brecv_ref[:, 0:LANES]
    second = brecv_ref[:, LANES : 2 * LANES]
    back = jnp.dot(sel_ref[0], first, preferred_element_type=F32)
    back = back + jnp.dot(sel_ref[1], second, preferred_element_type=F32)
    normed_grad = unstacked(back, tokens_here)
    column = iota((tokens_here, long), 1)
    scaled = []
    for k in range(2):
        at = routes[k] * GROUP + 8 + spots[k]
        found = jnp.dot(onehot(column == at), second, preferred_element_type=F32)
        scaled.append(found[:, 0:1] + found[:, LANES // 2 : LANES // 2 + 1])
    both = scaled[0] + scaled[1]
    logit_grad = jnp.zeros((tokens_here, peers), F32)
    for k in range(2):
        one = (1.0 - sigmoids[k]) * (scaled[k] - gates[k] * both)
        logit_grad = logit_grad + jnp.where(chosen[k], one, 0.0)
    for piece in pieces(logit_grad, 3):
        normed_grad = normed_grad + jnp.dot(piece, router, preferred_element_type=F32)
    token = token_ref[...]
    inner_grad = normed_grad * gain_ref[...]
    slope = total(inner_grad * token) * (scale * scale * scale * (1.0 / width))
    token_grad = cot_ref[...].astype(F32) + inner_grad * scale - token * slope
    values = [value_ref[pl.ds(i * tokens_here, tokens_here), :] for i in range(4)]
    hits = [total(token_grad * v) for v in values]
    pair_hit = [hits[0] + hits[1], hits[2] + hits[3]]
    quad_hit = pair_hit[0] + pair_hit[1]
    score_grads = []
    for i in range(4):
        grads = (0.25 * hits[i], 0.125 * pair_hit[i // 2], 0.0625 * quad_hit)
        mean = sum(a * g for a, g in zip(shares[i], grads))
        score_grads.append([a * (g - mean) for a, g in zip(shares[i], grads)])
    pair_grad = [score_grads[2 * h][1] + score_grads[2 * h + 1][1] for h in range(2)]
    quad_grad = sum(g[2] for g in score_grads)
    result = []
    for i in range(4):
        own_grad = score_grads[i][0] + 0.5 * pair_grad[i // 2] + 0.25 * quad_grad
        result.append((mix[i] * token_grad + own_grad * weight).astype(BF16))
    shuffle = onehot(order == lax.rem(place, tokens_here) * 4 + place // tokens_here)
    gemb_ref[...] = jnp.dot(
        shuffle, jnp.concatenate(result, axis=0), preferred_element_type=F32
    ).astype(BF16)
    exchange_end(*backward)


def per_device(
    byte_embed, score_weight, norm_gain, router, routes, expert_in, expert_out, cotangent
):
    steps, peers = lax.axis_size("seq"), lax.axis_size("exp")
    count, width = byte_embed.shape[1:]
    hidden = expert_in.shape[2]
    tokens_here = routes.shape[1]
    half = steps // 2
    slots = peers * CAP
    long = peers * GROUP
    parts = width // LANES
    vmem = pl.BlockSpec(memory_space=pltpu.VMEM)
    hbm = pl.BlockSpec(memory_space=pltpu.HBM)
    dma = pltpu.SemaphoreType.DMA
    gemb, gin, gout = pl.pallas_call(
        functools.partial(block_step, steps, peers),
        out_shape=(
            jax.ShapeDtypeStruct((count, width), BF16),
            jax.ShapeDtypeStruct((width, hidden), F32),
            jax.ShapeDtypeStruct((hidden, width), F32),
        ),
        in_specs=[hbm] * 8,
        out_specs=(vmem,) * 3,
        scratch_shapes=[
            pltpu.VMEM((count, width), BF16),
            pltpu.VMEM((tokens_here, width), BF16),
            pltpu.VMEM((width, hidden), BF16),
            pltpu.VMEM((hidden, width), BF16),
            pltpu.VMEM((1, width), F32),
            pltpu.VMEM((1, width), F32),
            pltpu.VMEM((peers, width), BF16),
            pltpu.VMEM((2, tokens_here), jnp.int32),
            pltpu.VMEM((count, width), F32),
            pltpu.VMEM((tokens_here, width), F32),
            pltpu.VMEM((long, 3 * LANES), BF16),
            pltpu.VMEM((long, 3 * LANES), BF16),
            pltpu.VMEM((long, 2 * LANES), BF16),
            pltpu.VMEM((long, 2 * LANES), BF16),
            pltpu.VMEM((2, parts * tokens_here, long), BF16),
            pltpu.VMEM((4, parts * 16 * CAP, 16 * GROUP), BF16),
            pltpu.VMEM((4 * 16 * CAP, 16 * GROUP), BF16),
            pltpu.VMEM((steps * tokens_here, (1 + 2 * SPREAD) * LANES), BF16),
            pltpu.VMEM((half * long, SPREAD * LANES), BF16),
            pltpu.VMEM((half * long, SPREAD * LANES), BF16),
            pltpu.VMEM((steps * slots, width), BF16),
            pltpu.VMEM((steps * slots, width), BF16),
            pltpu.VMEM((steps * slots, hidden), BF16),
            pltpu.VMEM((steps * slots, hidden), BF16),
            pltpu.VMEM((steps * slots, width), BF16),
            pltpu.VMEM((steps, 8, LANES), F32),
            pltpu.VMEM((steps * slots, width), BF16),
            pltpu.VMEM((steps * slots, width), BF16),
            pltpu.VMEM((steps, 8, LANES), F32),
            pltpu.VMEM((steps, 8, LANES), F32),
            dma((8,)),
            dma((peers,)),
            dma((peers,)),
            dma((peers,)),
            dma((peers,)),
            dma((2, half)),
            dma((2, half)),
            dma((half,)),
            dma((half,)),
            dma((2, half, 2)),
            dma((2, half, 2)),
            dma((2, half, slots // SPLIT)),
            dma((2, half, slots // SPLIT)),
            dma((2, half)),
            dma((2, half)),
        ],
        compiler_params=pltpu.CompilerParams(
            collective_id=0, has_side_effects=True, vmem_limit_bytes=52 * 1024 * 1024
        ),
    )(
        byte_embed[0],
        score_weight[None],
        norm_gain[None],
        router.T,
        routes[0].T,
        expert_in[0],
        expert_out[0],
        cotangent[0],
    )
    return (gemb[None], gin[None], gout[None])


def solution(mesh):
    in_specs = (
        P("exp", "seq", None),
        P(),
        P(),
        P(),
        P("exp", "seq", None),
        P("exp", None, "seq"),
        P("exp", "seq", None),
        P("exp", "seq", None),
    )
    out_specs = (P("exp", "seq", None), P("exp", None, "seq"), P("exp", "seq", None))
    return jax.shard_map(
        per_device, mesh=mesh, in_specs=in_specs, out_specs=out_specs, check_vma=False
    )
```

```python
import functools

import jax
import jax.numpy as jnp
from jax import lax
from jax.experimental import pallas as pl
from jax.experimental.pallas import tpu as pltpu
from jax.sharding import PartitionSpec as P

SQRT_HALF = 0.7071067811865476
INV_ROOT_TWO_PI = 0.3989422804014327
MESH = pl.DeviceIdType.MESH
LANES = 128
SPLIT = 16
SPREAD = 4
CAP = 3
GROUP = 16
ROWS = (((0,), (0,)), ((), ()))
COLS = (((1,), (1,)), ((), ()))
F32 = jnp.float32
BF16 = jnp.bfloat16


def pieces(value, count):
    out = []
    for _ in range(count):
        part = value.astype(BF16)
        out.append(part)
        value = value - part.astype(F32)
    return out


def stacked(value):
    parts = [value[:, at : at + LANES] for at in range(0, value.shape[1], LANES)]
    return jnp.concatenate(parts, axis=0)


def unstacked(value, rows):
    parts = [value[at : at + rows, :] for at in range(0, value.shape[0], rows)]
    return jnp.concatenate(parts, axis=1)


def total(value):
    return jnp.sum(value, axis=1, keepdims=True)


def iota(shape, dim):
    return lax.broadcasted_iota(jnp.int32, shape, dim)


def onehot(mask):
    return mask.astype(F32).astype(BF16)


def block_step(
    steps,
    peers,
    emb_hbm,
    score_hbm,
    gain_hbm,
    router_hbm,
    routes_hbm,
    win_hbm,
    wout_hbm,
    cot_hbm,
    gemb_ref,
    gin_ref,
    gout_ref,
    emb_ref,
    cot_ref,
    win_ref,
    wout_ref,
    score_ref,
    gain_ref,
    router_ref,
    routes_ref,
    value_ref,
    token_ref,
    send_ref,
    recv_ref,
    bsend_ref,
    brecv_ref,
    sel_ref,
    pick_ref,
    spread_ref,
    tb,
    tsend,
    trecv,
    xs,
    cs,
    hid,
    hgrad,
    part,
    gpart,
    take,
    give,
    gtake,
    ggive,
    in_sem,
    fx_send,
    fx_recv,
    bx_send,
    bx_recv,
    tb_send,
    tb_recv,
    tx_send,
    tx_recv,
    ag_send,
    ag_recv,
    rs_send,
    rs_recv,
    rg_send,
    rg_recv,
):
    me = lax.axis_index("seq")
    mine = lax.axis_index("exp")
    half = steps // 2
    right = lax.rem(me + 1, steps)
    left = lax.rem(me + steps - 1, steps)
    tokens_here, width = cot_ref.shape
    slots = peers * CAP
    parts = width // LANES
    block = width // half
    count_sub = slots // SPLIT
    early = (tuple(range(count_sub // 2)), tuple(range(count_sub // 2, count_sub)))
    fresh = early[::-1]
    wide_cols = SPREAD * LANES
    ring_cols = width - wide_cols

    loads = [
        pltpu.make_async_copy(src, dst, in_sem.at[at])
        for at, (src, dst) in enumerate(
            (
                (emb_hbm, emb_ref),
                (score_hbm, score_ref),
                (gain_hbm, gain_ref),
                (routes_hbm, routes_ref),
                (router_hbm, router_ref),
                (cot_hbm, cot_ref),
                (win_hbm, win_ref),
                (wout_hbm, wout_ref),
            )
        )
    ]
    for load in loads:
        load.start()

    barrier = pltpu.get_barrier_semaphore()
    for peer in (left, right):
        pl.semaphore_signal(barrier, inc=1, device_id={"seq": peer}, device_id_type=MESH)

    def greet(k, carry):
        pl.semaphore_signal(
            barrier, inc=1, device_id={"exp": lax.rem(mine + k, peers)}, device_id_type=MESH
        )
        return carry

    lax.fori_loop(1, peers, greet, 0)

    loads[0].wait()
    loads[1].wait()
    count = 4 * tokens_here
    order = iota((count, count), 0)
    place = iota((count, count), 1)
    shuffle = onehot(place == lax.rem(order, tokens_here) * 4 + order // tokens_here)
    value_ref[...] = jnp.dot(shuffle, emb_ref[...], preferred_element_type=F32)
    values = [value_ref[pl.ds(i * tokens_here, tokens_here), :] for i in range(4)]
    weight = score_ref[...]
    scores = [total(v * weight) for v in values]
    pair = [0.5 * (scores[0] + scores[1]), 0.5 * (scores[2] + scores[3])]
    quad = 0.5 * (pair[0] + pair[1])
    shares = []
    for i in range(4):
        three = (scores[i], pair[i // 2], quad)
        top = jnp.maximum(jnp.maximum(three[0], three[1]), three[2])
        raised = [jnp.exp(s - top) for s in three]
        bottom = raised[0] + raised[1] + raised[2]
        shares.append([r / bottom for r in raised])
    pair_share = [shares[2 * h][1] + shares[2 * h + 1][1] for h in range(2)]
    quad_share = shares[0][2] + shares[1][2] + shares[2][2] + shares[3][2]
    mix = [
        0.25 * (shares[i][0] + 0.5 * pair_share[i // 2] + 0.25 * quad_share) for i in range(4)
    ]
    token = mix[0] * values[0] + mix[1] * values[1] + mix[2] * values[2] + mix[3] * values[3]
    token_ref[...] = token
    scale = lax.rsqrt(total(token * token) * (1.0 / width) + 1e-06)
    for load in loads[2:6]:
        load.wait()
    normed = token * scale * gain_ref[...]
    sent = normed.astype(BF16)
    router = router_ref[...]
    logits = jnp.zeros((tokens_here, peers), F32)
    for piece in pieces(normed, 3):
        logits = logits + lax.dot_general(piece, router, COLS, preferred_element_type=F32)
    lane = iota((tokens_here, peers), 1)
    level = lane == iota((tokens_here, peers), 0)
    named = routes_ref[...].astype(F32)
    routes = [
        total(jnp.where(level, named[k : k + 1, :], 0.0)).astype(jnp.int32) for k in range(2)
    ]
    chosen = [lane == routes[k] for k in range(2)]
    picked = [total(jnp.where(hit, logits, 0.0)) for hit in chosen]
    sigmoids = [1.0 / (1.0 + jnp.exp(-v)) for v in picked]
    gates = [s / (sigmoids[0] + sigmoids[1]) for s in sigmoids]
    named = onehot(chosen[0]) + onehot(chosen[1])
    before = onehot(iota((tokens_here, tokens_here), 1) < iota((tokens_here, tokens_here), 0))
    earlier = jnp.dot(before, named, preferred_element_type=F32)
    spots = [total(jnp.where(hit, earlier, 0.0)).astype(jnp.int32) for hit in chosen]
    codes = [routes[k] * 4 + spots[k] for k in range(2)]

    tall = parts * tokens_here
    long = peers * GROUP
    column = iota((tall, long), 1)
    expert = column // GROUP
    inner = lax.rem(column, GROUP)
    upper = inner // 8
    piece_at = lax.rem(inner, 8)
    row_piece = iota((tall, 1), 0) // tokens_here
    row_codes = [jnp.concatenate([code] * parts, axis=0) * 8 + row_piece for code in codes]
    row_gates = [jnp.concatenate([gate] * parts, axis=0) for gate in gates]
    base = expert * 32 + piece_at
    wanted = (
        base + upper * 8,
        jnp.where(upper == 0, base + 16, -1),
        jnp.where(upper == 1, base, -1),
        base + 8 + upper * 8,
    )
    for at in range(2):
        hit = jnp.where(row_codes[0] == wanted[at], 1.0, 0.0)
        hit = hit + jnp.where(row_codes[1] == wanted[at], 1.0, 0.0)
        sel_ref[at] = hit.astype(BF16)
    sent_tall = stacked(sent)
    cot_tall = stacked(cot_ref[...])
    own = []
    for at in range(2):
        own.append(lax.dot_general(sel_ref[at], sent_tall, ROWS, preferred_element_type=F32))
    for at in range(2, 4):
        gated = jnp.where(row_codes[0] == wanted[at], row_gates[0], 0.0)
        gated = gated + jnp.where(row_codes[1] == wanted[at], row_gates[1], 0.0)
        high, low = pieces(gated, 2)
        one = lax.dot_general(high, cot_tall, ROWS, preferred_element_type=F32)
        own.append(one + lax.dot_general(low, cot_tall, ROWS, preferred_element_type=F32))
    send_ref[:, 0:LANES] = own[0].astype(BF16)
    send_ref[:, LANES : 2 * LANES] = (own[1] + own[2]).astype(BF16)
    send_ref[:, 2 * LANES : 3 * LANES] = own[3].astype(BF16)

    meta = jnp.zeros((tokens_here, LANES), F32)
    lane = iota((tokens_here, LANES), 1)
    for k in range(2):
        high, low = pieces(gates[k], 2)
        for at, column in enumerate((codes[k].astype(F32), high.astype(F32), low.astype(F32))):
            meta = jnp.where(lane == 2 * at + k, column, meta)

    def token_rows(index):
        return pl.ds(pl.multiple_of(index * tokens_here, tokens_here), tokens_here)

    tb[token_rows(me), 0:LANES] = meta.astype(BF16)
    tb[token_rows(me), LANES : LANES + wide_cols] = sent[:, ring_cols:]
    tb[token_rows(me), LANES + wide_cols :] = cot_ref[:, ring_cols:]

    def source(way, j):
        return lax.rem(me - j + steps, steps) if way == 0 else lax.rem(me + j, steps)

    def token_copy(way, j, index):
        cols = pl.ds(0, LANES + 2 * wide_cols)
        if isinstance(j, int) and j == half - 1:
            cols = pl.ds(LANES + wide_cols, wide_cols) if way else pl.ds(0, LANES + wide_cols)
        here = tb.at[token_rows(index), cols]
        return pltpu.make_async_remote_copy(
            src_ref=here,
            dst_ref=here,
            send_sem=tb_send.at[way, j],
            recv_sem=tb_recv.at[way, j],
            device_id={"seq": left if way else right},
            device_id_type=MESH,
        )

    def token_send(way, j):
        return token_copy(way, j, source(way, j))

    def token_arrival(way, j):
        return token_copy(way, j, source(way, j + 1))

    def spread_rows(j, start=0, size=long):
        return pl.ds(pl.multiple_of((j - 1) * long + start, 16), size)

    def spread_copy(j, k):
        peer = lax.rem(mine + k, peers)
        return pltpu.make_async_remote_copy(
            src_ref=tsend.at[spread_rows(j, peer * GROUP, GROUP)],
            dst_ref=trecv.at[spread_rows(j, mine * GROUP, GROUP)],
            send_sem=tx_send.at[j - 1],
            recv_sem=tx_recv.at[j - 1],
            device_id={"exp": peer},
            device_id_type=MESH,
        )

    def spread_all(j):
        size = (peers - 1) * GROUP
        return pltpu.make_async_remote_copy(
            src_ref=tsend.at[spread_rows(j, 0, size)],
            dst_ref=trecv.at[spread_rows(j, 0, size)],
            send_sem=tx_send.at[j - 1],
            recv_sem=tx_recv.at[j - 1],
            device_id={"exp": lax.rem(mine + 1, peers)},
            device_id_type=MESH,
        )

    def choose(index, offset):
        block = tb[token_rows(index), :]
        meta = block[:, 0:LANES].astype(F32)
        column = iota((tokens_here, long), 1)
        row = lax.rem(column, GROUP) - offset
        base = (column // GROUP) * 4
        for_x = jnp.where((row >= 0) & (row < CAP), base + row, -1).astype(F32)
        for_c = jnp.where((row >= CAP) & (row < 2 * CAP), base + row - CAP, -1).astype(F32)
        found = high = low = jnp.zeros((tokens_here, long), F32)
        for k in range(2):
            code = meta[:, k : k + 1]
            found = found + jnp.where(code == for_x, 1.0, 0.0)
            high = high + jnp.where(code == for_c, meta[:, 2 + k : 3 + k], 0.0)
            low = low + jnp.where(code == for_c, meta[:, 4 + k : 5 + k], 0.0)
        cot = block[:, LANES + wide_cols :]
        picks = [found.astype(BF16), high.astype(BF16), low.astype(BF16)]
        return picks, [block[:, LANES : LANES + wide_cols], cot, cot]

    def spread(j):
        picks, rows = choose(source(0, j), 0)
        if not (isinstance(j, int) and j == half):
            more_picks, more_rows = choose(source(1, j), 2 * CAP)
            picks, rows = picks + more_picks, rows + more_rows
        tsend[spread_rows(j), :] = lax.dot_general(
            jnp.concatenate(picks, axis=0),
            jnp.concatenate(rows, axis=0),
            ROWS,
            preferred_element_type=F32,
        ).astype(BF16)

        def start(k, carry):
            spread_copy(j, k).start()
            return carry

        lax.fori_loop(1, peers, start, 0)
        trecv[spread_rows(j, mine * GROUP, GROUP), :] = tsend[
            spread_rows(j, mine * GROUP, GROUP), :
        ]

    def token_step(j):
        for way in range(2):
            token_arrival(way, j - 1).wait_recv()
            if not (isinstance(j, int) and j == half):
                token_send(way, j).start()
        spread(j)

    pl.semaphore_wait(barrier, peers + 1)
    for way in range(2):
        token_send(way, 0).start()

    def group_rows(index):
        return pl.ds(pl.multiple_of(index * GROUP, GROUP), GROUP)

    def exchange(k, src_ref, dst_ref, send_sem, recv_sem):
        peer = lax.rem(mine + k, peers)
        return pltpu.make_async_remote_copy(
            src_ref=src_ref.at[group_rows(peer)],
            dst_ref=dst_ref.at[group_rows(mine)],
            send_sem=send_sem.at[k],
            recv_sem=recv_sem.at[k],
            device_id={"exp": peer},
            device_id_type=MESH,
        )

    def arrived(k, src_ref, dst_ref, send_sem, recv_sem):
        peer = lax.rem(mine + peers - k, peers)
        return pltpu.make_async_remote_copy(
            src_ref=src_ref.at[group_rows(peer)],
            dst_ref=dst_ref.at[group_rows(peer)],
            send_sem=send_sem.at[k],
            recv_sem=recv_sem.at[k],
            device_id={"exp": peer},
            device_id_type=MESH,
        )

    def exchange_start(*refs):
        def start(k, carry):
            exchange(k, *refs).start()
            return carry

        lax.fori_loop(1, peers, start, 0)
        refs[1][group_rows(mine), :] = refs[0][group_rows(mine), :]

    def exchange_wait(*refs):
        def wait(k, carry):
            arrived(k, *refs).wait_recv()
            return carry

        lax.fori_loop(1, peers, wait, 0)

    def exchange_end(*refs):
        def wait(k, carry):
            exchange(k, *refs).wait_send()
            return carry

        lax.fori_loop(1, peers, wait, 0)

    forward = (send_ref, recv_ref, fx_send, fx_recv)
    backward = (bsend_ref, brecv_ref, bx_send, bx_recv)
    exchange_start(*forward)

    near = 16
    few = near * CAP
    deep = parts * few
    wide = near * GROUP
    row = iota((deep, wide), 0)
    slot = lax.rem(row, few)
    inner = lax.rem(iota((deep, wide), 1), GROUP)
    same = (slot // CAP == iota((deep, wide), 1) // GROUP) & (lax.rem(inner, 8) == row // few)
    spot = lax.rem(slot, CAP)
    upper = inner // 8
    pick_ref[0] = onehot(same & (spot == upper))
    pick_ref[1] = onehot(same & (spot == 2) & (upper == 0))
    pick_ref[2] = onehot(same & (spot == 0) & (upper == 1))
    pick_ref[3] = onehot(same & (spot == 1 + upper))
    gpart[...] = jnp.zeros_like(gpart)
    row = iota((4 * few, wide), 0)
    column = iota((4 * few, wide), 1)
    slot = lax.rem(row, few)
    spread_ref[...] = onehot(
        (slot // CAP == column // GROUP)
        & (lax.rem(column, GROUP) == (row // few) * CAP + lax.rem(slot, CAP))
    )

    def rows_of(index, start=0, size=slots):
        return pl.ds(pl.multiple_of(index * slots + start, 16), size)

    def spread_in(j):
        spread_all(j).wait_recv()
        both = not (isinstance(j, int) and j == half)
        for at in range(peers // near):
            found = jnp.dot(
                spread_ref[...],
                trecv[spread_rows(j, at * wide, wide), :],
                preferred_element_type=F32,
            ).astype(BF16)
            for way in range(2 if both else 1):
                here = rows_of(source(way, j), at * few, few)
                base = 2 * way * few
                xs[here, ring_cols:] = found[base : base + few, :]
                cs[here, ring_cols:] = found[base + few : base + 2 * few, :]

    def gather(way, j, sub):
        buf = cs if sub else xs
        at = rows_of(source(way, j))
        return pltpu.make_async_remote_copy(
            src_ref=buf.at[at, pl.ds(0, ring_cols)],
            dst_ref=buf.at[at, pl.ds(0, ring_cols)],
            send_sem=ag_send.at[way, j, sub],
            recv_sem=ag_recv.at[way, j, sub],
            device_id={"seq": left if way else right},
            device_id_type=MESH,
        )

    def arrival(way, j, sub):
        buf = cs if sub else xs
        at = rows_of(source(way, j + 1))
        return pltpu.make_async_remote_copy(
            src_ref=buf.at[at, pl.ds(0, ring_cols)],
            dst_ref=buf.at[at, pl.ds(0, ring_cols)],
            send_sem=ag_send.at[way, j, sub],
            recv_sem=ag_recv.at[way, j, sub],
            device_id={"seq": left if way else right},
            device_id_type=MESH,
        )

    def target(way, s):
        return lax.rem(me + half - s, steps) if way == 0 else lax.rem(me + half + s, steps)

    def scatter(way, s, sub, direct=False):
        at = way * half + s
        here = rows_of(at, sub * SPLIT, SPLIT)
        src = part.at[rows_of(target(way, s), sub * SPLIT, SPLIT)] if direct else give.at[here]
        return pltpu.make_async_remote_copy(
            src_ref=src,
            dst_ref=take.at[here],
            send_sem=rs_send.at[way, s, sub],
            recv_sem=rs_recv.at[way, s, sub],
            device_id={"seq": left if way else right},
            device_id_type=MESH,
        )

    def scatter_gate(way, s, direct=False):
        at = way * half + s
        src = gpart.at[target(way, s)] if direct else ggive.at[at]
        return pltpu.make_async_remote_copy(
            src_ref=src,
            dst_ref=gtake.at[at],
            send_sem=rg_send.at[way, s],
            recv_sem=rg_recv.at[way, s],
            device_id={"seq": left if way else right},
            device_id_type=MESH,
        )

    def compute(index):
        at = rows_of(index)
        pre = jnp.dot(xs[at, :], win_ref[...], preferred_element_type=F32)
        up = lax.dot_general(cs[at, :], wout_ref[...], COLS, preferred_element_type=F32)
        cdf = 0.5 * (1.0 + lax.erf(pre * SQRT_HALF))
        pdf = INV_ROOT_TWO_PI * jnp.exp(-0.5 * pre * pre)
        hidden = pre * cdf
        hg = (up * (cdf + pre * pdf)).astype(BF16)
        hid[at, :] = hidden.astype(BF16)
        hgrad[at, :] = hg
        part[at, :] = lax.dot_general(
            hg, win_ref[...], COLS, preferred_element_type=F32
        ).astype(BF16)
        high, low = pieces(hidden * up, 2)
        ones = jnp.ones((8, high.shape[1]), BF16)
        terms = lax.dot_general(ones, high, COLS, preferred_element_type=F32)
        terms = terms + lax.dot_general(ones, low, COLS, preferred_element_type=F32)
        gpart[index, :, 0:slots] = terms

    token_step(1)
    token_step(2)
    exchange_wait(*forward)
    for sub, buf in enumerate((xs, cs)):
        for near_at in range(peers // near):
            here = recv_ref[pl.ds(near_at * wide, wide), :]
            lanes = sub * LANES
            one = jnp.dot(
                pick_ref[2 * sub], here[:, lanes : lanes + LANES], preferred_element_type=F32
            )
            two = jnp.dot(
                pick_ref[2 * sub + 1],
                here[:, lanes + LANES : lanes + 2 * LANES],
                preferred_element_type=F32,
            )
            buf[rows_of(me, near_at * few, few), :] = unstacked((one + two).astype(BF16), few)
        for way in range(2):
            gather(way, 0, sub).start()
    loads[6].wait()
    loads[7].wait()
    compute(me)

    def pass_on(j):
        for sub in range(2):
            for way in range(2):
                arrival(way, j - 1, sub).wait_recv()
                gather(way, j, sub).start()

    def ring_step(j, carry):
        token_step(j + 2)
        pass_on(j)
        spread_in(j)
        compute(source(0, j))
        compute(source(1, j))
        return carry

    lax.fori_loop(1, half - 3, ring_step, 0)
    last = half - 1
    ring_step(last - 2, 0)
    ring_step(last - 1, 0)
    for sub in range(2):
        for way in range(2):
            arrival(way, last - 1, sub).wait_recv()
            if sub == way:
                gather(way, last, sub).start()
    spread_in(last)
    for way in range(2):
        compute(source(way, last))
        for sub in fresh[1 - way]:
            scatter(1 - way, 1, sub, direct=True).start()
    scatter_gate(1, 1, direct=True).start()
    spread_in(half)
    arrival(0, last, 0).wait_recv()
    arrival(1, last, 1).wait_recv()
    compute(source(0, half))

    def weights(s):
        span = pl.ds(pl.multiple_of(s * block, LANES), block)
        gin_ref[span, :] = lax.dot_general(
            xs[:, span], hgrad[...], ROWS, preferred_element_type=F32
        )
        gout_ref[:, span] = lax.dot_general(
            hid[...], cs[:, span], ROWS, preferred_element_type=F32
        )

    def merge(way, s, sub):
        at = way * half + s
        ours = part[rows_of(target(way, s), sub * SPLIT, SPLIT), :].astype(F32)
        came = take[rows_of(at - 1, sub * SPLIT, SPLIT), :].astype(F32)
        give[rows_of(at, sub * SPLIT, SPLIT), :] = (ours + came).astype(BF16)

    for way in range(2):
        for sub in early[way]:
            scatter(way, 0, sub, direct=True).start()
    scatter_gate(0, 0, direct=True).start()
    weights(0)
    for at in range(len(early[0])):
        for way in range(2):
            sub = early[way][at]
            scatter(way, 0, sub, direct=True).wait_recv()
            merge(way, 1, sub)
            scatter(way, 1, sub).start()
    scatter_gate(0, 0, direct=True).wait_recv()
    ggive[1] = gpart[target(0, 1)] + gtake[0]
    scatter_gate(0, 1).start()
    weights(1)

    def scatter_step(s, carry):
        for at in range(count_sub):
            for way in range(2):
                sub = (fresh[way] + early[way])[at]
                scatter(way, s - 1, sub).wait_recv()
                merge(way, s, sub)
                scatter(way, s, sub).start()
        for way in range(2):
            scatter_gate(way, s - 1).wait_recv()
            at = way * half + s
            ggive[at] = gpart[target(way, s)] + gtake[at - 1]
            scatter_gate(way, s).start()
        weights(s)
        return carry

    lax.fori_loop(2, half, scatter_step, 0)

    summed = []
    for sub in range(count_sub):
        whole = part[rows_of(me, sub * SPLIT, SPLIT), :].astype(F32)
        for way in range(2):
            scatter(way, last, sub).wait_recv()
            whole = whole + take[rows_of(way * half + last, sub * SPLIT, SPLIT), :].astype(F32)
        summed.append(whole.astype(BF16))
    each = count_sub * near // peers
    summed = [jnp.concatenate(summed[at : at + each], axis=0) for at in range(0, count_sub, each)]
    terms = gpart[me]
    for way in range(2):
        scatter_gate(way, last).wait_recv()
        terms = terms + gtake[way * half + last]

    for near_at in range(peers // near):
        tall_rows = stacked(summed[near_at])
        here = pl.ds(near_at * wide, wide)
        for at in range(2):
            bsend_ref[here, pl.ds(at * LANES, LANES)] = lax.dot_general(
                pick_ref[at], tall_rows, ROWS, preferred_element_type=F32
            ).astype(BF16)
    row = iota((long, LANES), 0)
    column = iota((long, LANES), 1)
    fits = (column // CAP == row // GROUP) & (
        lax.rem(row, GROUP) == 8 + lax.rem(column, CAP)
    )
    spread = total(jnp.where(fits & (column < slots), terms[0:1, :], 0.0))
    high, low = pieces(spread, 2)
    two = jnp.where(column < LANES // 2, high.astype(F32), low.astype(F32))
    kept = bsend_ref[:, LANES : 2 * LANES].astype(F32)
    bsend_ref[:, LANES : 2 * LANES] = (kept + two).astype(BF16)
    exchange_start(*backward)
    exchange_end(*forward)
    for way in range(2):
        for s in range(half):
            token_send(way, s).wait_send()
            if way == 0:
                spread_all(s + 1).wait_send()
            for sub in range(2):
                if s < last or sub == way:
                    gather(way, s, sub).wait_send()
            for sub in range(count_sub):
                if s >= 1 or sub in early[way]:
                    scatter(way, s, sub).wait_send()
            if s >= 1 or way == 0:
                scatter_gate(way, s).wait_send()
    exchange_wait(*backward)

    first = brecv_ref[:, 0:LANES]
    second = brecv_ref[:, LANES : 2 * LANES]
    back = jnp.dot(sel_ref[0], first, preferred_element_type=F32)
    back = back + jnp.dot(sel_ref[1], second, preferred_element_type=F32)
    normed_grad = unstacked(back, tokens_here)
    column = iota((tokens_here, long), 1)
    scaled = []
    for k in range(2):
        at = routes[k] * GROUP + 8 + spots[k]
        found = jnp.dot(onehot(column == at), second, preferred_element_type=F32)
        scaled.append(found[:, 0:1] + found[:, LANES // 2 : LANES // 2 + 1])
    both = scaled[0] + scaled[1]
    logit_grad = jnp.zeros((tokens_here, peers), F32)
    for k in range(2):
        one = (1.0 - sigmoids[k]) * (scaled[k] - gates[k] * both)
        logit_grad = logit_grad + jnp.where(chosen[k], one, 0.0)
    for piece in pieces(logit_grad, 3):
        normed_grad = normed_grad + jnp.dot(piece, router, preferred_element_type=F32)
    token = token_ref[...]
    inner_grad = normed_grad * gain_ref[...]
    slope = total(inner_grad * token) * (scale * scale * scale * (1.0 / width))
    token_grad = cot_ref[...].astype(F32) + inner_grad * scale - token * slope
    values = [value_ref[pl.ds(i * tokens_here, tokens_here), :] for i in range(4)]
    hits = [total(token_grad * v) for v in values]
    pair_hit = [hits[0] + hits[1], hits[2] + hits[3]]
    quad_hit = pair_hit[0] + pair_hit[1]
    score_grads = []
    for i in range(4):
        grads = (0.25 * hits[i], 0.125 * pair_hit[i // 2], 0.0625 * quad_hit)
        mean = sum(a * g for a, g in zip(shares[i], grads))
        score_grads.append([a * (g - mean) for a, g in zip(shares[i], grads)])
    pair_grad = [score_grads[2 * h][1] + score_grads[2 * h + 1][1] for h in range(2)]
    quad_grad = sum(g[2] for g in score_grads)
    result = []
    for i in range(4):
        own_grad = score_grads[i][0] + 0.5 * pair_grad[i // 2] + 0.25 * quad_grad
        result.append((mix[i] * token_grad + own_grad * weight).astype(BF16))
    shuffle = onehot(order == lax.rem(place, tokens_here) * 4 + place // tokens_here)
    gemb_ref[...] = jnp.dot(
        shuffle, jnp.concatenate(result, axis=0), preferred_element_type=F32
    ).astype(BF16)
    exchange_end(*backward)


def per_device(
    byte_embed, score_weight, norm_gain, router, routes, expert_in, expert_out, cotangent
):
    steps, peers = lax.axis_size("seq"), lax.axis_size("exp")
    count, width = byte_embed.shape[1:]
    hidden = expert_in.shape[2]
    tokens_here = routes.shape[1]
    half = steps // 2
    slots = peers * CAP
    long = peers * GROUP
    parts = width // LANES
    vmem = pl.BlockSpec(memory_space=pltpu.VMEM)
    hbm = pl.BlockSpec(memory_space=pltpu.HBM)
    dma = pltpu.SemaphoreType.DMA
    gemb, gin, gout = pl.pallas_call(
        functools.partial(block_step, steps, peers),
        out_shape=(
            jax.ShapeDtypeStruct((count, width), BF16),
            jax.ShapeDtypeStruct((width, hidden), F32),
            jax.ShapeDtypeStruct((hidden, width), F32),
        ),
        in_specs=[hbm] * 8,
        out_specs=(vmem,) * 3,
        scratch_shapes=[
            pltpu.VMEM((count, width), BF16),
            pltpu.VMEM((tokens_here, width), BF16),
            pltpu.VMEM((width, hidden), BF16),
            pltpu.VMEM((hidden, width), BF16),
            pltpu.VMEM((1, width), F32),
            pltpu.VMEM((1, width), F32),
            pltpu.VMEM((peers, width), BF16),
            pltpu.VMEM((2, tokens_here), jnp.int32),
            pltpu.VMEM((count, width), F32),
            pltpu.VMEM((tokens_here, width), F32),
            pltpu.VMEM((long, 3 * LANES), BF16),
            pltpu.VMEM((long, 3 * LANES), BF16),
            pltpu.VMEM((long, 2 * LANES), BF16),
            pltpu.VMEM((long, 2 * LANES), BF16),
            pltpu.VMEM((2, parts * tokens_here, long), BF16),
            pltpu.VMEM((4, parts * 16 * CAP, 16 * GROUP), BF16),
            pltpu.VMEM((4 * 16 * CAP, 16 * GROUP), BF16),
            pltpu.VMEM((steps * tokens_here, (1 + 2 * SPREAD) * LANES), BF16),
            pltpu.VMEM((half * long, SPREAD * LANES), BF16),
            pltpu.VMEM((half * long, SPREAD * LANES), BF16),
            pltpu.VMEM((steps * slots, width), BF16),
            pltpu.VMEM((steps * slots, width), BF16),
            pltpu.VMEM((steps * slots, hidden), BF16),
            pltpu.VMEM((steps * slots, hidden), BF16),
            pltpu.VMEM((steps * slots, width), BF16),
            pltpu.VMEM((steps, 8, LANES), F32),
            pltpu.VMEM((steps * slots, width), BF16),
            pltpu.VMEM((steps * slots, width), BF16),
            pltpu.VMEM((steps, 8, LANES), F32),
            pltpu.VMEM((steps, 8, LANES), F32),
            dma((8,)),
            dma((peers,)),
            dma((peers,)),
            dma((peers,)),
            dma((peers,)),
            dma((2, half)),
            dma((2, half)),
            dma((half,)),
            dma((half,)),
            dma((2, half, 2)),
            dma((2, half, 2)),
            dma((2, half, slots // SPLIT)),
            dma((2, half, slots // SPLIT)),
            dma((2, half)),
            dma((2, half)),
        ],
        compiler_params=pltpu.CompilerParams(
            collective_id=0, has_side_effects=True, vmem_limit_bytes=67043328
        ),
    )(
        byte_embed[0],
        score_weight[None],
        norm_gain[None],
        router.T,
        routes[0].T,
        expert_in[0],
        expert_out[0],
        cotangent[0],
    )
    return (gemb[None], gin[None], gout[None])


def solution(mesh):
    in_specs = (
        P("exp", "seq", None),
        P(),
        P(),
        P(),
        P("exp", "seq", None),
        P("exp", None, "seq"),
        P("exp", "seq", None),
        P("exp", "seq", None),
    )
    out_specs = (P("exp", "seq", None), P("exp", None, "seq"), P("exp", "seq", None))
    return jax.shard_map(
        per_device, mesh=mesh, in_specs=in_specs, out_specs=out_specs, check_vma=False
    )
```

```python
import functools

import jax
import jax.numpy as jnp
from jax import lax
from jax.experimental import pallas as pl
from jax.experimental.pallas import tpu as pltpu
from jax.sharding import PartitionSpec as P

SQRT_HALF = 0.7071067811865476
INV_ROOT_TWO_PI = 0.3989422804014327
MESH = pl.DeviceIdType.MESH
LANES = 128
SPLIT = 16
SPREAD = 4
CAP = 3
GROUP = 16
ROWS = (((0,), (0,)), ((), ()))
COLS = (((1,), (1,)), ((), ()))
F32 = jnp.float32
BF16 = jnp.bfloat16


def pieces(value, count):
    out = []
    for _ in range(count):
        part = value.astype(BF16)
        out.append(part)
        value = value - part.astype(F32)
    return out


def stacked(value):
    parts = [value[:, at : at + LANES] for at in range(0, value.shape[1], LANES)]
    return jnp.concatenate(parts, axis=0)


def unstacked(value, rows):
    parts = [value[at : at + rows, :] for at in range(0, value.shape[0], rows)]
    return jnp.concatenate(parts, axis=1)


def total(value):
    return jnp.sum(value, axis=1, keepdims=True)


def iota(shape, dim):
    return lax.broadcasted_iota(jnp.int32, shape, dim)


def onehot(mask):
    return mask.astype(F32).astype(BF16)


def block_step(
    steps,
    peers,
    emb_hbm,
    score_hbm,
    gain_hbm,
    router_hbm,
    routes_hbm,
    win_hbm,
    wout_hbm,
    cot_hbm,
    gemb_ref,
    gin_hbm,
    gout_hbm,
    gin_ref,
    gout_ref,
    emb_ref,
    cot_ref,
    win_ref,
    wout_ref,
    score_ref,
    gain_ref,
    router_ref,
    routes_ref,
    value_ref,
    token_ref,
    send_ref,
    recv_ref,
    bsend_ref,
    brecv_ref,
    sel_ref,
    pick_ref,
    spread_ref,
    tb,
    tsend,
    trecv,
    xs,
    cs,
    hid,
    hgrad,
    part,
    gpart,
    take,
    give,
    gtake,
    ggive,
    in_sem,
    fx_send,
    fx_recv,
    bx_send,
    bx_recv,
    tb_send,
    tb_recv,
    tx_send,
    tx_recv,
    ag_send,
    ag_recv,
    rs_send,
    rs_recv,
    rg_send,
    rg_recv,
):
    me = lax.axis_index("seq")
    mine = lax.axis_index("exp")
    half = steps // 2
    right = lax.rem(me + 1, steps)
    left = lax.rem(me + steps - 1, steps)
    tokens_here, width = cot_ref.shape
    slots = peers * CAP
    parts = width // LANES
    block = width // half
    count_sub = slots // SPLIT
    early = (tuple(range(count_sub // 2)), tuple(range(count_sub // 2, count_sub)))
    fresh = early[::-1]
    wide_cols = SPREAD * LANES
    ring_cols = width - wide_cols

    loads = [
        pltpu.make_async_copy(src, dst, in_sem.at[at])
        for at, (src, dst) in enumerate(
            (
                (emb_hbm, emb_ref),
                (score_hbm, score_ref),
                (gain_hbm, gain_ref),
                (routes_hbm, routes_ref),
                (router_hbm, router_ref),
                (cot_hbm, cot_ref),
                (win_hbm, win_ref),
                (wout_hbm, wout_ref),
            )
        )
    ]
    for load in loads:
        load.start()

    barrier = pltpu.get_barrier_semaphore()
    for peer in (left, right):
        pl.semaphore_signal(barrier, inc=1, device_id={"seq": peer}, device_id_type=MESH)

    def greet(k, carry):
        pl.semaphore_signal(
            barrier, inc=1, device_id={"exp": lax.rem(mine + k, peers)}, device_id_type=MESH
        )
        return carry

    lax.fori_loop(1, peers, greet, 0)

    loads[0].wait()
    loads[1].wait()
    count = 4 * tokens_here
    order = iota((count, count), 0)
    place = iota((count, count), 1)
    shuffle = onehot(place == lax.rem(order, tokens_here) * 4 + order // tokens_here)
    value_ref[...] = jnp.dot(shuffle, emb_ref[...], preferred_element_type=F32)
    values = [value_ref[pl.ds(i * tokens_here, tokens_here), :] for i in range(4)]
    weight = score_ref[...]
    scores = [total(v * weight) for v in values]
    pair = [0.5 * (scores[0] + scores[1]), 0.5 * (scores[2] + scores[3])]
    quad = 0.5 * (pair[0] + pair[1])
    shares = []
    for i in range(4):
        three = (scores[i], pair[i // 2], quad)
        top = jnp.maximum(jnp.maximum(three[0], three[1]), three[2])
        raised = [jnp.exp(s - top) for s in three]
        bottom = raised[0] + raised[1] + raised[2]
        shares.append([r / bottom for r in raised])
    pair_share = [shares[2 * h][1] + shares[2 * h + 1][1] for h in range(2)]
    quad_share = shares[0][2] + shares[1][2] + shares[2][2] + shares[3][2]
    mix = [
        0.25 * (shares[i][0] + 0.5 * pair_share[i // 2] + 0.25 * quad_share) for i in range(4)
    ]
    token = mix[0] * values[0] + mix[1] * values[1] + mix[2] * values[2] + mix[3] * values[3]
    token_ref[...] = token
    scale = lax.rsqrt(total(token * token) * (1.0 / width) + 1e-06)
    for load in loads[2:6]:
        load.wait()
    normed = token * scale * gain_ref[...]
    sent = normed.astype(BF16)
    router = router_ref[...]
    logits = jnp.zeros((tokens_here, peers), F32)
    for piece in pieces(normed, 3):
        logits = logits + lax.dot_general(piece, router, COLS, preferred_element_type=F32)
    lane = iota((tokens_here, peers), 1)
    level = lane == iota((tokens_here, peers), 0)
    named = routes_ref[...].astype(F32)
    routes = [
        total(jnp.where(level, named[k : k + 1, :], 0.0)).astype(jnp.int32) for k in range(2)
    ]
    chosen = [lane == routes[k] for k in range(2)]
    picked = [total(jnp.where(hit, logits, 0.0)) for hit in chosen]
    sigmoids = [1.0 / (1.0 + jnp.exp(-v)) for v in picked]
    gates = [s / (sigmoids[0] + sigmoids[1]) for s in sigmoids]
    named = onehot(chosen[0]) + onehot(chosen[1])
    before = onehot(iota((tokens_here, tokens_here), 1) < iota((tokens_here, tokens_here), 0))
    earlier = jnp.dot(before, named, preferred_element_type=F32)
    spots = [total(jnp.where(hit, earlier, 0.0)).astype(jnp.int32) for hit in chosen]
    codes = [routes[k] * 4 + spots[k] for k in range(2)]

    tall = parts * tokens_here
    long = peers * GROUP
    column = iota((tall, long), 1)
    expert = column // GROUP
    inner = lax.rem(column, GROUP)
    upper = inner // 8
    piece_at = lax.rem(inner, 8)
    row_piece = iota((tall, 1), 0) // tokens_here
    row_codes = [jnp.concatenate([code] * parts, axis=0) * 8 + row_piece for code in codes]
    row_gates = [jnp.concatenate([gate] * parts, axis=0) for gate in gates]
    base = expert * 32 + piece_at
    wanted = (
        base + upper * 8,
        jnp.where(upper == 0, base + 16, -1),
        jnp.where(upper == 1, base, -1),
        base + 8 + upper * 8,
    )
    for at in range(2):
        hit = jnp.where(row_codes[0] == wanted[at], 1.0, 0.0)
        hit = hit + jnp.where(row_codes[1] == wanted[at], 1.0, 0.0)
        sel_ref[at] = hit.astype(BF16)
    sent_tall = stacked(sent)
    cot_tall = stacked(cot_ref[...])
    own = []
    for at in range(2):
        own.append(lax.dot_general(sel_ref[at], sent_tall, ROWS, preferred_element_type=F32))
    for at in range(2, 4):
        gated = jnp.where(row_codes[0] == wanted[at], row_gates[0], 0.0)
        gated = gated + jnp.where(row_codes[1] == wanted[at], row_gates[1], 0.0)
        high, low = pieces(gated, 2)
        one = lax.dot_general(high, cot_tall, ROWS, preferred_element_type=F32)
        own.append(one + lax.dot_general(low, cot_tall, ROWS, preferred_element_type=F32))
    send_ref[:, 0:LANES] = own[0].astype(BF16)
    send_ref[:, LANES : 2 * LANES] = (own[1] + own[2]).astype(BF16)
    send_ref[:, 2 * LANES : 3 * LANES] = own[3].astype(BF16)

    meta = jnp.zeros((tokens_here, LANES), F32)
    lane = iota((tokens_here, LANES), 1)
    for k in range(2):
        high, low = pieces(gates[k], 2)
        for at, column in enumerate((codes[k].astype(F32), high.astype(F32), low.astype(F32))):
            meta = jnp.where(lane == 2 * at + k, column, meta)

    def token_rows(index):
        return pl.ds(pl.multiple_of(index * tokens_here, tokens_here), tokens_here)

    tb[token_rows(me), 0:LANES] = meta.astype(BF16)
    tb[token_rows(me), LANES : LANES + wide_cols] = sent[:, ring_cols:]
    tb[token_rows(me), LANES + wide_cols :] = cot_ref[:, ring_cols:]

    def source(way, j):
        return lax.rem(me - j + steps, steps) if way == 0 else lax.rem(me + j, steps)

    def token_copy(way, j, index):
        cols = pl.ds(0, LANES + 2 * wide_cols)
        if isinstance(j, int) and j == half - 1:
            cols = pl.ds(LANES + wide_cols, wide_cols) if way else pl.ds(0, LANES + wide_cols)
        here = tb.at[token_rows(index), cols]
        return pltpu.make_async_remote_copy(
            src_ref=here,
            dst_ref=here,
            send_sem=tb_send.at[way, j],
            recv_sem=tb_recv.at[way, j],
            device_id={"seq": left if way else right},
            device_id_type=MESH,
        )

    def token_send(way, j):
        return token_copy(way, j, source(way, j))

    def token_arrival(way, j):
        return token_copy(way, j, source(way, j + 1))

    def spread_rows(j, start=0, size=long):
        return pl.ds(pl.multiple_of((j - 1) * long + start, 16), size)

    def spread_copy(j, k):
        peer = lax.rem(mine + k, peers)
        return pltpu.make_async_remote_copy(
            src_ref=tsend.at[spread_rows(j, peer * GROUP, GROUP)],
            dst_ref=trecv.at[spread_rows(j, mine * GROUP, GROUP)],
            send_sem=tx_send.at[j - 1],
            recv_sem=tx_recv.at[j - 1],
            device_id={"exp": peer},
            device_id_type=MESH,
        )

    def spread_all(j):
        size = (peers - 1) * GROUP
        return pltpu.make_async_remote_copy(
            src_ref=tsend.at[spread_rows(j, 0, size)],
            dst_ref=trecv.at[spread_rows(j, 0, size)],
            send_sem=tx_send.at[j - 1],
            recv_sem=tx_recv.at[j - 1],
            device_id={"exp": lax.rem(mine + 1, peers)},
            device_id_type=MESH,
        )

    def choose(index, offset):
        block = tb[token_rows(index), :]
        meta = block[:, 0:LANES].astype(F32)
        column = iota((tokens_here, long), 1)
        row = lax.rem(column, GROUP) - offset
        base = (column // GROUP) * 4
        for_x = jnp.where((row >= 0) & (row < CAP), base + row, -1).astype(F32)
        for_c = jnp.where((row >= CAP) & (row < 2 * CAP), base + row - CAP, -1).astype(F32)
        found = high = low = jnp.zeros((tokens_here, long), F32)
        for k in range(2):
            code = meta[:, k : k + 1]
            found = found + jnp.where(code == for_x, 1.0, 0.0)
            high = high + jnp.where(code == for_c, meta[:, 2 + k : 3 + k], 0.0)
            low = low + jnp.where(code == for_c, meta[:, 4 + k : 5 + k], 0.0)
        cot = block[:, LANES + wide_cols :]
        picks = [found.astype(BF16), high.astype(BF16), low.astype(BF16)]
        return picks, [block[:, LANES : LANES + wide_cols], cot, cot]

    def spread(j):
        picks, rows = choose(source(0, j), 0)
        if not (isinstance(j, int) and j == half):
            more_picks, more_rows = choose(source(1, j), 2 * CAP)
            picks, rows = picks + more_picks, rows + more_rows
        tsend[spread_rows(j), :] = lax.dot_general(
            jnp.concatenate(picks, axis=0),
            jnp.concatenate(rows, axis=0),
            ROWS,
            preferred_element_type=F32,
        ).astype(BF16)

        def start(k, carry):
            spread_copy(j, k).start()
            return carry

        lax.fori_loop(1, peers, start, 0)
        trecv[spread_rows(j, mine * GROUP, GROUP), :] = tsend[
            spread_rows(j, mine * GROUP, GROUP), :
        ]

    def token_step(j):
        for way in range(2):
            token_arrival(way, j - 1).wait_recv()
            if not (isinstance(j, int) and j == half):
                token_send(way, j).start()
        spread(j)

    pl.semaphore_wait(barrier, peers + 1)
    for way in range(2):
        token_send(way, 0).start()

    def group_rows(index):
        return pl.ds(pl.multiple_of(index * GROUP, GROUP), GROUP)

    def exchange(k, src_ref, dst_ref, send_sem, recv_sem):
        peer = lax.rem(mine + k, peers)
        return pltpu.make_async_remote_copy(
            src_ref=src_ref.at[group_rows(peer)],
            dst_ref=dst_ref.at[group_rows(mine)],
            send_sem=send_sem.at[k],
            recv_sem=recv_sem.at[k],
            device_id={"exp": peer},
            device_id_type=MESH,
        )

    def arrived(k, src_ref, dst_ref, send_sem, recv_sem):
        peer = lax.rem(mine + peers - k, peers)
        return pltpu.make_async_remote_copy(
            src_ref=src_ref.at[group_rows(peer)],
            dst_ref=dst_ref.at[group_rows(peer)],
            send_sem=send_sem.at[k],
            recv_sem=recv_sem.at[k],
            device_id={"exp": peer},
            device_id_type=MESH,
        )

    def exchange_start(*refs):
        def start(k, carry):
            exchange(k, *refs).start()
            return carry

        lax.fori_loop(1, peers, start, 0)
        refs[1][group_rows(mine), :] = refs[0][group_rows(mine), :]

    def exchange_wait(*refs):
        def wait(k, carry):
            arrived(k, *refs).wait_recv()
            return carry

        lax.fori_loop(1, peers, wait, 0)

    def exchange_end(*refs):
        def wait(k, carry):
            exchange(k, *refs).wait_send()
            return carry

        lax.fori_loop(1, peers, wait, 0)

    forward = (send_ref, recv_ref, fx_send, fx_recv)
    backward = (bsend_ref, brecv_ref, bx_send, bx_recv)
    exchange_start(*forward)

    near = 16
    few = near * CAP
    deep = parts * few
    wide = near * GROUP
    row = iota((deep, wide), 0)
    slot = lax.rem(row, few)
    inner = lax.rem(iota((deep, wide), 1), GROUP)
    same = (slot // CAP == iota((deep, wide), 1) // GROUP) & (lax.rem(inner, 8) == row // few)
    spot = lax.rem(slot, CAP)
    upper = inner // 8
    pick_ref[0] = onehot(same & (spot == upper))
    pick_ref[1] = onehot(same & (spot == 2) & (upper == 0))
    pick_ref[2] = onehot(same & (spot == 0) & (upper == 1))
    pick_ref[3] = onehot(same & (spot == 1 + upper))
    gpart[...] = jnp.zeros_like(gpart)
    row = iota((4 * few, wide), 0)
    column = iota((4 * few, wide), 1)
    slot = lax.rem(row, few)
    spread_ref[...] = onehot(
        (slot // CAP == column // GROUP)
        & (lax.rem(column, GROUP) == (row // few) * CAP + lax.rem(slot, CAP))
    )

    def rows_of(index, start=0, size=slots):
        return pl.ds(pl.multiple_of(index * slots + start, 16), size)

    def spread_in(j):
        spread_all(j).wait_recv()
        both = not (isinstance(j, int) and j == half)
        for at in range(peers // near):
            found = jnp.dot(
                spread_ref[...],
                trecv[spread_rows(j, at * wide, wide), :],
                preferred_element_type=F32,
            ).astype(BF16)
            for way in range(2 if both else 1):
                here = rows_of(source(way, j), at * few, few)
                base = 2 * way * few
                xs[here, ring_cols:] = found[base : base + few, :]
                cs[here, ring_cols:] = found[base + few : base + 2 * few, :]

    def gather(way, j, sub):
        buf = cs if sub else xs
        at = rows_of(source(way, j))
        return pltpu.make_async_remote_copy(
            src_ref=buf.at[at, pl.ds(0, ring_cols)],
            dst_ref=buf.at[at, pl.ds(0, ring_cols)],
            send_sem=ag_send.at[way, j, sub],
            recv_sem=ag_recv.at[way, j, sub],
            device_id={"seq": left if way else right},
            device_id_type=MESH,
        )

    def arrival(way, j, sub):
        buf = cs if sub else xs
        at = rows_of(source(way, j + 1))
        return pltpu.make_async_remote_copy(
            src_ref=buf.at[at, pl.ds(0, ring_cols)],
            dst_ref=buf.at[at, pl.ds(0, ring_cols)],
            send_sem=ag_send.at[way, j, sub],
            recv_sem=ag_recv.at[way, j, sub],
            device_id={"seq": left if way else right},
            device_id_type=MESH,
        )

    def target(way, s):
        return lax.rem(me + half - s, steps) if way == 0 else lax.rem(me + half + s, steps)

    def scatter(way, s, sub, direct=False):
        at = way * half + s
        here = rows_of(at, sub * SPLIT, SPLIT)
        src = part.at[rows_of(target(way, s), sub * SPLIT, SPLIT)] if direct else give.at[here]
        return pltpu.make_async_remote_copy(
            src_ref=src,
            dst_ref=take.at[here],
            send_sem=rs_send.at[way, s, sub],
            recv_sem=rs_recv.at[way, s, sub],
            device_id={"seq": left if way else right},
            device_id_type=MESH,
        )

    def scatter_gate(way, s, direct=False):
        at = way * half + s
        src = gpart.at[target(way, s)] if direct else ggive.at[at]
        return pltpu.make_async_remote_copy(
            src_ref=src,
            dst_ref=gtake.at[at],
            send_sem=rg_send.at[way, s],
            recv_sem=rg_recv.at[way, s],
            device_id={"seq": left if way else right},
            device_id_type=MESH,
        )

    def compute(index):
        at = rows_of(index)
        pre = jnp.dot(xs[at, :], win_ref[...], preferred_element_type=F32)
        up = lax.dot_general(cs[at, :], wout_ref[...], COLS, preferred_element_type=F32)
        cdf = 0.5 * (1.0 + lax.erf(pre * SQRT_HALF))
        pdf = INV_ROOT_TWO_PI * jnp.exp(-0.5 * pre * pre)
        hidden = pre * cdf
        hg = (up * (cdf + pre * pdf)).astype(BF16)
        hid[at, :] = hidden.astype(BF16)
        hgrad[at, :] = hg
        part[at, :] = lax.dot_general(
            hg, win_ref[...], COLS, preferred_element_type=F32
        ).astype(BF16)
        high, low = pieces(hidden * up, 2)
        ones = jnp.ones((8, high.shape[1]), BF16)
        terms = lax.dot_general(ones, high, COLS, preferred_element_type=F32)
        terms = terms + lax.dot_general(ones, low, COLS, preferred_element_type=F32)
        gpart[index, :, 0:slots] = terms

    token_step(1)
    token_step(2)
    exchange_wait(*forward)
    for sub, buf in enumerate((xs, cs)):
        for near_at in range(peers // near):
            here = recv_ref[pl.ds(near_at * wide, wide), :]
            lanes = sub * LANES
            one = jnp.dot(
                pick_ref[2 * sub], here[:, lanes : lanes + LANES], preferred_element_type=F32
            )
            two = jnp.dot(
                pick_ref[2 * sub + 1],
                here[:, lanes + LANES : lanes + 2 * LANES],
                preferred_element_type=F32,
            )
            buf[rows_of(me, near_at * few, few), :] = unstacked((one + two).astype(BF16), few)
        for way in range(2):
            gather(way, 0, sub).start()
    loads[6].wait()
    loads[7].wait()
    compute(me)

    def pass_on(j):
        for sub in range(2):
            for way in range(2):
                arrival(way, j - 1, sub).wait_recv()
                gather(way, j, sub).start()

    def ring_step(j, carry):
        token_step(j + 2)
        pass_on(j)
        spread_in(j)
        compute(source(0, j))
        compute(source(1, j))
        return carry

    lax.fori_loop(1, half - 3, ring_step, 0)
    last = half - 1
    ring_step(last - 2, 0)
    ring_step(last - 1, 0)
    for sub in range(2):
        for way in range(2):
            arrival(way, last - 1, sub).wait_recv()
            if sub == way:
                gather(way, last, sub).start()
    spread_in(last)
    for way in range(2):
        compute(source(way, last))
        for sub in fresh[1 - way]:
            scatter(1 - way, 1, sub, direct=True).start()
    scatter_gate(1, 1, direct=True).start()
    spread_in(half)
    arrival(0, last, 0).wait_recv()
    arrival(1, last, 1).wait_recv()
    compute(source(0, half))

    def weights(s):
        span = pl.ds(pl.multiple_of(s * block, LANES), block)
        gin_ref[span, :] = lax.dot_general(
            xs[:, span], hgrad[...], ROWS, preferred_element_type=F32
        )
        gout_ref[:, span] = lax.dot_general(
            hid[...], cs[:, span], ROWS, preferred_element_type=F32
        )

    def merge(way, s, sub):
        at = way * half + s
        ours = part[rows_of(target(way, s), sub * SPLIT, SPLIT), :].astype(F32)
        came = take[rows_of(at - 1, sub * SPLIT, SPLIT), :].astype(F32)
        give[rows_of(at, sub * SPLIT, SPLIT), :] = (ours + came).astype(BF16)

    for way in range(2):
        for sub in early[way]:
            scatter(way, 0, sub, direct=True).start()
    scatter_gate(0, 0, direct=True).start()
    weights(0)
    for at in range(len(early[0])):
        for way in range(2):
            sub = early[way][at]
            scatter(way, 0, sub, direct=True).wait_recv()
            merge(way, 1, sub)
            scatter(way, 1, sub).start()
    scatter_gate(0, 0, direct=True).wait_recv()
    ggive[1] = gpart[target(0, 1)] + gtake[0]
    scatter_gate(0, 1).start()
    weights(1)

    def scatter_step(s, carry):
        for at in range(count_sub):
            for way in range(2):
                sub = (fresh[way] + early[way])[at]
                scatter(way, s - 1, sub).wait_recv()
                merge(way, s, sub)
                scatter(way, s, sub).start()
        for way in range(2):
            scatter_gate(way, s - 1).wait_recv()
            at = way * half + s
            ggive[at] = gpart[target(way, s)] + gtake[at - 1]
            scatter_gate(way, s).start()
        weights(s)
        return carry

    lax.fori_loop(2, half, scatter_step, 0)
    stores = [
        pltpu.make_async_copy(src, dst, in_sem.at[at])
        for at, (src, dst) in enumerate(((gin_ref, gin_hbm), (gout_ref, gout_hbm)))
    ]
    for store in stores:
        store.start()

    summed = []
    for sub in range(count_sub):
        whole = part[rows_of(me, sub * SPLIT, SPLIT), :].astype(F32)
        for way in range(2):
            scatter(way, last, sub).wait_recv()
            whole = whole + take[rows_of(way * half + last, sub * SPLIT, SPLIT), :].astype(F32)
        summed.append(whole.astype(BF16))
    each = count_sub * near // peers
    summed = [jnp.concatenate(summed[at : at + each], axis=0) for at in range(0, count_sub, each)]
    terms = gpart[me]
    for way in range(2):
        scatter_gate(way, last).wait_recv()
        terms = terms + gtake[way * half + last]

    for near_at in range(peers // near):
        tall_rows = stacked(summed[near_at])
        here = pl.ds(near_at * wide, wide)
        for at in range(2):
            bsend_ref[here, pl.ds(at * LANES, LANES)] = lax.dot_general(
                pick_ref[at], tall_rows, ROWS, preferred_element_type=F32
            ).astype(BF16)
    row = iota((long, LANES), 0)
    column = iota((long, LANES), 1)
    fits = (column // CAP == row // GROUP) & (
        lax.rem(row, GROUP) == 8 + lax.rem(column, CAP)
    )
    spread = total(jnp.where(fits & (column < slots), terms[0:1, :], 0.0))
    high, low = pieces(spread, 2)
    two = jnp.where(column < LANES // 2, high.astype(F32), low.astype(F32))
    kept = bsend_ref[:, LANES : 2 * LANES].astype(F32)
    bsend_ref[:, LANES : 2 * LANES] = (kept + two).astype(BF16)
    exchange_start(*backward)
    exchange_end(*forward)
    for way in range(2):
        for s in range(half):
            token_send(way, s).wait_send()
            if way == 0:
                spread_all(s + 1).wait_send()
            for sub in range(2):
                if s < last or sub == way:
                    gather(way, s, sub).wait_send()
            for sub in range(count_sub):
                if s >= 1 or sub in early[way]:
                    scatter(way, s, sub).wait_send()
            if s >= 1 or way == 0:
                scatter_gate(way, s).wait_send()
    exchange_wait(*backward)

    first = brecv_ref[:, 0:LANES]
    second = brecv_ref[:, LANES : 2 * LANES]
    back = jnp.dot(sel_ref[0], first, preferred_element_type=F32)
    back = back + jnp.dot(sel_ref[1], second, preferred_element_type=F32)
    normed_grad = unstacked(back, tokens_here)
    column = iota((tokens_here, long), 1)
    scaled = []
    for k in range(2):
        at = routes[k] * GROUP + 8 + spots[k]
        found = jnp.dot(onehot(column == at), second, preferred_element_type=F32)
        scaled.append(found[:, 0:1] + found[:, LANES // 2 : LANES // 2 + 1])
    both = scaled[0] + scaled[1]
    logit_grad = jnp.zeros((tokens_here, peers), F32)
    for k in range(2):
        one = (1.0 - sigmoids[k]) * (scaled[k] - gates[k] * both)
        logit_grad = logit_grad + jnp.where(chosen[k], one, 0.0)
    for piece in pieces(logit_grad, 3):
        normed_grad = normed_grad + jnp.dot(piece, router, preferred_element_type=F32)
    token = token_ref[...]
    inner_grad = normed_grad * gain_ref[...]
    slope = total(inner_grad * token) * (scale * scale * scale * (1.0 / width))
    token_grad = cot_ref[...].astype(F32) + inner_grad * scale - token * slope
    values = [value_ref[pl.ds(i * tokens_here, tokens_here), :] for i in range(4)]
    hits = [total(token_grad * v) for v in values]
    pair_hit = [hits[0] + hits[1], hits[2] + hits[3]]
    quad_hit = pair_hit[0] + pair_hit[1]
    score_grads = []
    for i in range(4):
        grads = (0.25 * hits[i], 0.125 * pair_hit[i // 2], 0.0625 * quad_hit)
        mean = sum(a * g for a, g in zip(shares[i], grads))
        score_grads.append([a * (g - mean) for a, g in zip(shares[i], grads)])
    pair_grad = [score_grads[2 * h][1] + score_grads[2 * h + 1][1] for h in range(2)]
    quad_grad = sum(g[2] for g in score_grads)
    result = []
    for i in range(4):
        own_grad = score_grads[i][0] + 0.5 * pair_grad[i // 2] + 0.25 * quad_grad
        result.append((mix[i] * token_grad + own_grad * weight).astype(BF16))
    shuffle = onehot(order == lax.rem(place, tokens_here) * 4 + place // tokens_here)
    gemb_ref[...] = jnp.dot(
        shuffle, jnp.concatenate(result, axis=0), preferred_element_type=F32
    ).astype(BF16)
    exchange_end(*backward)
    for store in stores:
        store.wait()


def hand_on(count, *refs):
    sources, results, buffers = refs[:count], refs[count : 2 * count], refs[2 * count : -2]
    load_sem, store_sem = refs[-2:]
    loads, stores = [], []
    for source, result, buffer in zip(sources, results, buffers):
        rows = min(source.shape[0], 128)
        for start in range(0, source.shape[0], rows):
            span, at = pl.ds(start, rows), len(loads)
            loads.append(
                pltpu.make_async_copy(source.at[span], buffer.at[span], load_sem.at[at])
            )
            stores.append(
                pltpu.make_async_copy(buffer.at[span], result.at[span], store_sem.at[at])
            )
    for load in loads:
        load.start()
    for load, store in zip(loads, stores):
        load.wait()
        store.start()
    for store in stores:
        store.wait()


def handed_on(*arrays):
    hbm = pl.BlockSpec(memory_space=pltpu.HBM)
    pieces_all = sum(-(-a.shape[0] // 128) for a in arrays)
    return pl.pallas_call(
        functools.partial(hand_on, len(arrays)),
        out_shape=tuple(jax.ShapeDtypeStruct(a.shape, a.dtype) for a in arrays),
        in_specs=[hbm] * len(arrays),
        out_specs=(hbm,) * len(arrays),
        scratch_shapes=[pltpu.VMEM(a.shape, a.dtype) for a in arrays]
        + [pltpu.SemaphoreType.DMA((pieces_all,))] * 2,
        compiler_params=pltpu.CompilerParams(vmem_limit_bytes=67043328),
    )(*arrays)


def per_device(
    byte_embed, score_weight, norm_gain, router, routes, expert_in, expert_out, cotangent
):
    steps, peers = lax.axis_size("seq"), lax.axis_size("exp")
    count, width = byte_embed.shape[1:]
    hidden = expert_in.shape[2]
    tokens_here = routes.shape[1]
    half = steps // 2
    slots = peers * CAP
    long = peers * GROUP
    parts = width // LANES
    vmem = pl.BlockSpec(memory_space=pltpu.VMEM)
    hbm = pl.BlockSpec(memory_space=pltpu.HBM)
    dma = pltpu.SemaphoreType.DMA
    gemb, gin, gout = pl.pallas_call(
        functools.partial(block_step, steps, peers),
        out_shape=(
            jax.ShapeDtypeStruct((count, width), BF16),
            jax.ShapeDtypeStruct((width, hidden), F32),
            jax.ShapeDtypeStruct((hidden, width), F32),
        ),
        in_specs=[hbm] * 8,
        out_specs=(vmem, hbm, hbm),
        scratch_shapes=[
            pltpu.VMEM((width, hidden), F32),
            pltpu.VMEM((hidden, width), F32),
            pltpu.VMEM((count, width), BF16),
            pltpu.VMEM((tokens_here, width), BF16),
            pltpu.VMEM((width, hidden), BF16),
            pltpu.VMEM((hidden, width), BF16),
            pltpu.VMEM((1, width), F32),
            pltpu.VMEM((1, width), F32),
            pltpu.VMEM((peers, width), BF16),
            pltpu.VMEM((2, tokens_here), jnp.int32),
            pltpu.VMEM((count, width), F32),
            pltpu.VMEM((tokens_here, width), F32),
            pltpu.VMEM((long, 3 * LANES), BF16),
            pltpu.VMEM((long, 3 * LANES), BF16),
            pltpu.VMEM((long, 2 * LANES), BF16),
            pltpu.VMEM((long, 2 * LANES), BF16),
            pltpu.VMEM((2, parts * tokens_here, long), BF16),
            pltpu.VMEM((4, parts * 16 * CAP, 16 * GROUP), BF16),
            pltpu.VMEM((4 * 16 * CAP, 16 * GROUP), BF16),
            pltpu.VMEM((steps * tokens_here, (1 + 2 * SPREAD) * LANES), BF16),
            pltpu.VMEM((half * long, SPREAD * LANES), BF16),
            pltpu.VMEM((half * long, SPREAD * LANES), BF16),
            pltpu.VMEM((steps * slots, width), BF16),
            pltpu.VMEM((steps * slots, width), BF16),
            pltpu.VMEM((steps * slots, hidden), BF16),
            pltpu.VMEM((steps * slots, hidden), BF16),
            pltpu.VMEM((steps * slots, width), BF16),
            pltpu.VMEM((steps, 8, LANES), F32),
            pltpu.VMEM((steps * slots, width), BF16),
            pltpu.VMEM((steps * slots, width), BF16),
            pltpu.VMEM((steps, 8, LANES), F32),
            pltpu.VMEM((steps, 8, LANES), F32),
            dma((8,)),
            dma((peers,)),
            dma((peers,)),
            dma((peers,)),
            dma((peers,)),
            dma((2, half)),
            dma((2, half)),
            dma((half,)),
            dma((half,)),
            dma((2, half, 2)),
            dma((2, half, 2)),
            dma((2, half, slots // SPLIT)),
            dma((2, half, slots // SPLIT)),
            dma((2, half)),
            dma((2, half)),
        ],
        compiler_params=pltpu.CompilerParams(
            collective_id=0, has_side_effects=True, vmem_limit_bytes=67043328
        ),
    )(
        byte_embed[0],
        score_weight[None],
        norm_gain[None],
        router.T,
        routes[0].T,
        expert_in[0],
        expert_out[0],
        cotangent[0],
    )
    gin, gout, gemb = handed_on(gin, gout, gemb)
    return (gemb[None], gin[None], gout[None])


def solution(mesh):
    in_specs = (
        P("exp", "seq", None),
        P(),
        P(),
        P(),
        P("exp", "seq", None),
        P("exp", None, "seq"),
        P("exp", "seq", None),
        P("exp", "seq", None),
    )
    out_specs = (P("exp", "seq", None), P("exp", None, "seq"), P("exp", "seq", None))
    return jax.shard_map(
        per_device, mesh=mesh, in_specs=in_specs, out_specs=out_specs, check_vma=False
    )
```
